32 devices in a mesh: dp: 32 (over z, y, x, core).
Axes of the slice: x: 2, y: 2, z: 4, core: 2. Of those that a mesh axis runs over, the one named last changes fastest.
Arguments:
- events: bfloat16 [32768, 512], P('dp'), may hold values from -6 to 6
- home_slot: int32 [32768], P('dp'), may hold values from 0 to 1024, as said below
- dest_slot: int32 [32768], P('dp'), may hold values from 0 to 1024, as said below
- seq_lens: int32 [64], P('dp'), may hold values from 0 to 1024, as said below
- weights: bfloat16 [512, 2560], replicated, may hold values from -0.25 to 0.25
- out_grad: bfloat16 [32768, 512], P('dp'), may hold values from -6 to 6
- momentum_in: float32 [512, 2048], P('dp'), may hold values from -3 to 3
- momentum_out: float32 [512, 512], P('dp'), may hold values from -3 to 3
Outputs:
- event_grad: bfloat16 [32768, 512], P('dp')
- new_momentum_in: float32 [512, 2048], P('dp')
- new_momentum_out: float32 [512, 512], P('dp')
The draws below stay inside these ranges and needn't reach their ends.
Inputs may be any that keep to these rules, and one draw needn't show every extreme that they name: `seq_lens`: each device's 2 entries are the lengths of the sequences placed on it, in order, then zeros; the sequences' blocks, ceil(length / 512) each, add up to at most 2. `dest_slot`: for each row of a device's blocks: 1024 if the row lies in no sequence, else s * 32 + k, where s is the device that holds the row's event at home and k its slot among the rows that s sends to this device; no value below 1024 repeats on a device. `home_slot`: for each home row: 1024 if no sequence uses it, else t * 32 + k, where t is the device that takes the row and k its slot as in dest_slot; no value below 1024 repeats on a device, and the two arrays name the same rows. A device sends at most 32 rows to one device, and in every draw some device receives 32 rows from every device.
All inputs are finite; a program needn't handle non-finite values.
Results may differ from the reference program's by a relative error of at most 0.0085.
Values may be sent and summed in bfloat16 or wider, within the bound.
A program may use at most 128 MiB of HBM per device.

```python
import jax
import jax.numpy as jnp
from jax import lax

D = 512
HEADS = 8
BLK = 512
NBLK = 2
DEV_ROWS = 1024
ROWS = 32768


def row_owner_drawn(lengths, row_count):
    blocks = (lengths + BLK - 1) // BLK
    starts = (jnp.cumsum(blocks) - blocks) * BLK
    places = jnp.arange(row_count, dtype=jnp.int32)
    inside = (places[:, None] >= starts[None, :]) & (places[:, None] < starts[None, :] + lengths[None, :])
    labels = jnp.arange(lengths.shape[0], dtype=jnp.int32) + 1
    return (jnp.sum(jnp.where(inside, labels[None, :], 0), axis=1) - 1).astype(jnp.int32)


def placement_plan(base_key):
    devices = ROWS // DEV_ROWS
    capacity = DEV_ROWS // devices
    subkeys = jax.random.split(jax.random.fold_in(base_key, 7177), 6)
    device_ids = jnp.arange(devices, dtype=jnp.int32)
    block_ids = jnp.arange(NBLK, dtype=jnp.int32)
    used_blocks = jax.random.randint(subkeys[0], (devices,), (NBLK + 1) // 2, NBLK + 1, dtype=jnp.int32)
    crowded = jax.random.randint(subkeys[1], (), 0, devices, dtype=jnp.int32)
    used_blocks = jnp.where(device_ids == crowded, NBLK, used_blocks)
    breaks = jax.random.randint(subkeys[2], (devices, NBLK), 0, 2, dtype=jnp.int32)
    in_use = block_ids[None, :] < used_blocks[:, None]
    begins = jnp.where(block_ids[None, :] == 0, 1, breaks) * in_use.astype(jnp.int32)
    sequence_ids = (jnp.cumsum(begins, axis=1) - 1).astype(jnp.int32)
    matches = (sequence_ids[:, :, None] == block_ids[None, None, :]) & in_use[:, :, None]
    counts = jnp.sum(matches.astype(jnp.int32), axis=1).astype(jnp.int32)
    tail_rows = jax.random.randint(subkeys[3], (devices, NBLK), 1, BLK + 1, dtype=jnp.int32)
    tail_rows = jnp.where((device_ids == crowded)[:, None], BLK, tail_rows)
    lengths = jnp.where(counts > 0, (counts - 1) * BLK + tail_rows, 0).astype(jnp.int32)
    owners = jax.vmap(lambda entry: row_owner_drawn(entry, DEV_ROWS))(lengths)
    live_rows = (owners >= 0).astype(jnp.int32)
    rank_order = (jnp.cumsum(live_rows, axis=1) - 1).astype(jnp.int32)
    groups = jnp.clip(rank_order // capacity, 0, devices - 1)
    within = rank_order % capacity
    offsets = jax.random.permutation(subkeys[4], devices).astype(jnp.int32)
    sources = (device_ids[:, None] + offsets[groups]) % devices
    dest_slot = jnp.where(live_rows > 0, sources * capacity + within, DEV_ROWS).astype(jnp.int32)
    totals = jnp.sum(live_rows, axis=1).astype(jnp.int32)
    places = jnp.arange(DEV_ROWS, dtype=jnp.int32)
    place_group = places // capacity
    place_within = places % capacity
    targets = (device_ids[:, None] - offsets[place_group][None, :]) % devices
    values = jnp.where(places[None, :] < totals[targets], targets * capacity + place_within[None, :], DEV_ROWS).astype(jnp.int32)
    orders = jax.vmap(lambda subkey: jax.random.permutation(subkey, DEV_ROWS))(jax.random.split(subkeys[5], devices)).astype(jnp.int32)
    home_slot = jnp.zeros((devices, DEV_ROWS), jnp.int32).at[device_ids[:, None], orders].set(values)
    return (lengths, home_slot, dest_slot)


def draw_seq_lens(key, part):
    return placement_plan(key)[0].reshape(-1)


def draw_home_slot(key, part):
    return placement_plan(key)[1].reshape(-1)


def draw_dest_slot(key, part):
    return placement_plan(key)[2].reshape(-1)


def steps_of(rng, extent, cuts, smallest, largest):
    def one(dim, shards_of):
        steps = jax.random.uniform(jax.random.fold_in(jax.random.fold_in(rng, 6), dim), (shards_of,), jnp.float32, smallest / len(cuts), largest / len(cuts))
        return jnp.repeat(jnp.exp(steps), extent[dim] // shards_of).reshape((-1,) + (1,) * (len(extent) - dim - 1))

    level = one(*cuts[0])
    for cut in cuts[1:]:
        level = level * one(*cut)
    return level


def bell_draw(stream_key, dims, scale, most, cuts=(), kind=jnp.bfloat16):
    array = jax.random.normal(stream_key, dims, jnp.float32) * scale
    if len(cuts) > 0:
        array = steps_of(stream_key, dims, cuts, -0.22, 0.18) * array
    return jnp.clip(array, min=-most, max=most).astype(kind)


def setup_inputs(seed: int = 0) -> dict:
    streams_of = jax.random.split(jax.random.key(seed), 9)
    events = bell_draw(streams_of[0], (ROWS, D), 1.0, 6.0, ((0, 32),))
    home_slot = draw_home_slot(jax.random.fold_in(streams_of[8], 71), 0)
    dest_slot = draw_dest_slot(jax.random.fold_in(streams_of[8], 71), 0)
    seq_lens = draw_seq_lens(jax.random.fold_in(streams_of[8], 71), 0)
    weights = bell_draw(streams_of[4], (D, 5 * D), D ** -0.5, 0.25)
    out_grad = bell_draw(streams_of[5], (ROWS, D), 1.0, 6.0, ((0, 32),))
    momentum_in = bell_draw(streams_of[6], (D, 4 * D), 0.5, 3.0, ((0, 32),), jnp.float32)
    momentum_out = bell_draw(streams_of[7], (D, D), 0.5, 3.0, ((0, 32),), jnp.float32)
    return {"events": events, "home_slot": home_slot, "dest_slot": dest_slot, "seq_lens": seq_lens, "weights": weights, "out_grad": out_grad, "momentum_in": momentum_in, "momentum_out": momentum_out}


NORM_EPS = 1e-05
DECAY = 0.9

def row_owner(lengths, row_count):
    blocks = (lengths + BLK - 1) // BLK
    starts = (jnp.cumsum(blocks) - blocks) * BLK
    places = jnp.arange(row_count, dtype=jnp.int32)
    inside = (places[:, None] >= starts[None, :]) & (places[:, None] < starts[None, :] + lengths[None, :])
    labels = jnp.arange(lengths.shape[0], dtype=jnp.int32) + 1
    return (lax.optimization_barrier(jnp.sum(jnp.where(inside, labels[None, :], 0), axis=1)) - 1).astype(jnp.int32)

def attend_pair(queries, key_rows, value_rows, query_owner, key_owner, query_place, key_place):
    factor = queries.shape[2] ** (-0.5)
    scores = jnp.einsum('qhe,khe->hqk', queries.astype(jnp.float32), key_rows.astype(jnp.float32)) * factor
    allowed = (query_owner[:, None] == key_owner[None, :]) & (query_owner[:, None] >= 0) & (key_place[None, :] <= query_place[:, None])
    weights = jnp.where(allowed[None], jax.nn.silu(scores), 0.0).astype(jnp.bfloat16)
    return jnp.einsum('hqk,khe->qhe', weights.astype(jnp.float32), value_rows.astype(jnp.float32))

def mixing(hidden, owners):
    activated = jax.nn.silu(hidden)
    model_width = hidden.shape[1] // 4
    row_count = hidden.shape[0]
    head_size = model_width // HEADS
    gate_part = activated[:, :model_width]
    value_set = activated[:, model_width:2 * model_width].astype(jnp.bfloat16).reshape(row_count, HEADS, head_size)
    query_set = activated[:, 2 * model_width:3 * model_width].astype(jnp.bfloat16).reshape(row_count, HEADS, head_size)
    key_set = activated[:, 3 * model_width:].astype(jnp.bfloat16).reshape(row_count, HEADS, head_size)
    places = jnp.arange(row_count, dtype=jnp.int32)
    pieces = []
    for qblock in range(row_count // BLK):
        low_row = qblock * BLK
        high_row = low_row + BLK
        pieces.append(jax.checkpoint(attend_pair)(query_set[low_row:high_row], key_set[:high_row], value_set[:high_row], owners[low_row:high_row], owners[:high_row], places[low_row:high_row], places[:high_row]))
    attended = jnp.concatenate(pieces, axis=0).reshape(row_count, model_width)
    centre = lax.optimization_barrier(jnp.mean(attended, axis=1, keepdims=True))
    centred = attended - centre
    spread = lax.optimization_barrier(jnp.mean(centred * centred, axis=1, keepdims=True))
    return centred * lax.rsqrt(spread + NORM_EPS) * gate_part

def device_grads(tokens, upstream, weights, lengths):
    model_width = tokens.shape[1]
    owners = row_owner(lengths, tokens.shape[0])
    w_in = weights[:, :4 * model_width]
    w_out = weights[:, 4 * model_width:]
    hidden = jnp.dot(tokens, w_in, preferred_element_type=jnp.float32)
    mixed_out, pullback = jax.vjp(lambda hidden_in: mixing(hidden_in, owners), hidden)
    mixed_low = mixed_out.astype(jnp.bfloat16)
    mixed_grad = jnp.dot(upstream, w_out.T, preferred_element_type=jnp.float32)
    hidden_grad = pullback(mixed_grad)[0].astype(jnp.bfloat16)
    token_grad = (upstream.astype(jnp.float32) + jnp.dot(hidden_grad, w_in.T, preferred_element_type=jnp.float32)).astype(jnp.bfloat16)
    in_term = jnp.dot(tokens.T, hidden_grad, preferred_element_type=jnp.float32)
    out_term = jnp.dot(mixed_low.T, upstream, preferred_element_type=jnp.float32)
    return (token_grad, in_term, out_term)

def reference(events, home_slot, dest_slot, seq_lens, weights, out_grad, momentum_in, momentum_out):
    devices = ROWS // DEV_ROWS
    capacity = DEV_ROWS // devices
    model_width = events.shape[1]
    row_ids = jnp.arange(ROWS, dtype=jnp.int32)
    device_of = (row_ids // DEV_ROWS).astype(jnp.int32)
    send_keys = jnp.where(home_slot < DEV_ROWS, device_of * DEV_ROWS + home_slot, ROWS).astype(jnp.int32)
    lookup_table = jnp.full((ROWS + 1,), ROWS, dtype=jnp.int32).at[send_keys].set(row_ids)
    lookup_table = jnp.concatenate([lookup_table[:ROWS], jnp.full((1,), ROWS, dtype=jnp.int32)])
    receive_keys = jnp.where(dest_slot < DEV_ROWS, dest_slot // capacity * DEV_ROWS + device_of * capacity + dest_slot % capacity, ROWS).astype(jnp.int32)
    sources = lookup_table[receive_keys]
    padded = jnp.concatenate([events, jnp.zeros((1, model_width), jnp.bfloat16)], axis=0)
    tokens = padded[sources]

    def visit_device(running, entries):
        token_grad, in_term, out_term = device_grads(entries[0], entries[1], weights, entries[2])
        return ((running[0] + in_term, running[1] + out_term), token_grad)
    initial = (jnp.zeros((model_width, 4 * model_width), jnp.float32), jnp.zeros((model_width, model_width), jnp.float32))
    sums, token_grads = lax.scan(visit_device, initial, (tokens.reshape(devices, DEV_ROWS, model_width), out_grad.reshape(devices, DEV_ROWS, model_width), seq_lens.reshape(devices, NBLK)))
    event_grad = jnp.zeros((ROWS + 1, model_width), jnp.bfloat16).at[sources].set(token_grads.reshape(ROWS, model_width))[:ROWS]
    grad_scale = ROWS ** (-0.5)
    return (event_grad, DECAY * momentum_in + grad_scale * sums[0], DECAY * momentum_out + grad_scale * sums[1])
```

```python
import functools

import jax
import jax.numpy as jnp
from jax import lax
from jax.experimental import pallas as pl
from jax.experimental.pallas import tpu as pltpu
from jax.sharding import PartitionSpec as P

HEADS = 8
BLK = 512
QB = 256
PAIR = 128
NORM_EPS = 1e-05
DECAY = 0.9
MESH = pl.DeviceIdType.MESH
F32 = jnp.float32
BF16 = jnp.bfloat16
VMEM_LIMIT = 67 * 1000 * 1000
LAG = 2


def dot_nn(a, b):
    return lax.dot_general(a, b, (((1,), (0,)), ((), ())), preferred_element_type=F32)


def dot_nt(a, b):
    return lax.dot_general(a, b, (((1,), (1,)), ((), ())), preferred_element_type=F32)


def chain_bits(bit_count, second):
    order = list(range(bit_count))
    if second and bit_count > 2:
        order[1], order[2] = order[2], order[1]
    return order


def slot_device(slot, n, bits):
    return sum(((slot // (n >> (rank + 1))) % 2) << bit for rank, bit in enumerate(bits))


def enter_all(n, me):
    barrier = pltpu.get_barrier_semaphore()

    def greet(i, carry):
        pl.semaphore_signal(barrier, inc=1, device_id=((me + i) % n,), device_id_type=MESH)
        return carry

    lax.fori_loop(1, n, greet, 0)
    return barrier


def flip(value, other, size):
    total = 0
    weight = 1
    while weight < size:
        total = total + (value // weight + other // weight) % 2 * weight
        weight *= 2
    return total


class Exchange:
    def __init__(self, n, me, group, src, dst, ssem, rsem):
        self.n, self.me, self.group = n, me, group
        self.src, self.dst, self.ssem, self.rsem = src, dst, ssem, rsem

    def chunk(self, k):
        return flip(self.me // self.group, k, self.n // self.group)

    def each(self, k, act):
        base = self.chunk(k) * self.group
        low = self.me % self.group

        def go(j, carry):
            peer = base + flip(low, j, self.group)
            i = k * self.group + j
            act(
                pltpu.make_async_remote_copy(
                    src_ref=self.src.at[peer],
                    dst_ref=self.dst.at[self.me],
                    send_sem=self.ssem.at[i],
                    recv_sem=self.rsem.at[i],
                    device_id=(peer,),
                    device_id_type=MESH,
                )
            )
            return carry

        lax.fori_loop(1 if k == 0 else 0, self.group, go, 0)

    def start(self, k):
        self.each(k, lambda copy: copy.start())

    def finish(self, k):
        self.each(k, lambda copy: copy.wait())


def gather_matrix(slots_ref, out_ref):
    rows = out_ref.shape[0]
    wide = jnp.broadcast_to(slots_ref[...].astype(F32), (128, rows))
    column = jnp.transpose(wide)
    lane = lax.broadcasted_iota(jnp.int32, (rows, 128), 1).astype(F32)
    for j in range(rows // 128):
        out_ref[:, j * 128 : (j + 1) * 128] = jnp.where(
            column == lane + float(j * 128), 1.0, 0.0
        ).astype(BF16)


def scatter_chunk(slots_ref, start, size):
    rows = slots_ref.shape[1]
    place = lax.broadcasted_iota(jnp.int32, (size, rows), 0) + start
    return jnp.where(place == slots_ref[...], 1.0, 0.0).astype(BF16)


def same_owner(lens_ref, low, high):
    start = 0
    same = 0
    for j in range(lens_ref.shape[0]):
        blocks = (lens_ref[j] + BLK - 1) // BLK
        inside = jnp.where((start <= low) & (high < start + blocks), 1, 0)
        same = same + inside
        start = start + blocks
    return same


def order_block(height, base, width, n, per, bits, fold, turn):
    shape = (height, width)
    tall = per * fold
    place = lax.broadcasted_iota(jnp.int32, shape, 0) + base
    column = lax.broadcasted_iota(jnp.int32, shape, 1)
    slot = place // tall
    rest = place % tall
    device = jnp.zeros(shape, jnp.int32)
    for rank, bit in enumerate(bits):
        weight = n >> (rank + 1)
        device = device + ((slot // weight) % 2) * (1 << bit)
    hit = (column == device * per + rest % per) & (rest // per == turn)
    return jnp.where(hit, 1.0, 0.0).astype(BF16)


def step_kernel(n, scale, direct, lens_ref, home_ref, dest_ref, ev_ref, w_hbm, og_hbm, *refs):
    if direct:
        mi_ref, mo_ref, out_ev, ni_ref, no_ref, *refs = refs
        sums = None
    else:
        out_ev, *refs = refs
        sums, refs = refs[:4], refs[4:]
    (
        w_ref, og_ref, og_t, outbox, inbox, inbox2, pick, place, tok, tok_t, dmix_t,
        slope_t, gate_t, v_t, q_t, k_t, k_z, v_z, attn, slopes, att_t, hgrad_t, mixed_t,
        dout_t, acc, cross, lsem, ssem, rsem, ssem2, rsem2, hs, hr, *bufs,
    ) = refs
    me = lax.axis_index("dp")
    rows, width = ev_ref.shape
    cap = rows // n
    per = width // n
    fold = max(1, 16 // per)
    nq = rows // QB
    bits = n.bit_length() - 1
    group = QB // cap
    head = width // HEADS
    pairs = width // PAIR
    two = PAIR // head
    barrier = enter_all(n, me)
    load_w = pltpu.make_async_copy(w_hbm, w_ref, lsem.at[0])
    load_og = pltpu.make_async_copy(og_hbm, og_ref, lsem.at[1])
    load_w.start()
    load_og.start()
    there = Exchange(n, me, group, outbox, inbox, ssem, rsem)
    back = Exchange(n, me, group, outbox, inbox2, ssem2, rsem2)

    for k in range(nq):
        at = there.chunk(k)
        part = dot_nn(scatter_chunk(home_ref, at * QB, QB), ev_ref[...]).astype(BF16)
        outbox[pl.ds(at * group, group)] = part.reshape(group, cap, width)
        if k == 0:
            pl.semaphore_wait(barrier, n - 1)
        there.start(k)
    inbox[me] = outbox[me]
    gather_matrix(dest_ref, pick)
    load_w.wait()
    load_og.wait()

    def prepare(c, carry):
        r = pl.ds(pl.multiple_of(c * QB, QB), QB)
        place[r, :] = scatter_chunk(dest_ref, c * QB, QB)
        x = og_ref[r, :]
        og_t[:, r] = jnp.transpose(x)
        dmix_t[:, r] = (dot_nt(w_ref[:, 4 * width :], x) * 0.5).astype(BF16)
        return carry

    lax.fori_loop(0, nq, prepare, 0)

    def turn_w(c, carry):
        r = pl.ds(pl.multiple_of(c * QB, QB), QB)
        hgrad_t[r, :width] = jnp.transpose(w_ref[:, r]) * 0.5
        return carry

    lax.fori_loop(0, 4 * width // QB, turn_w, 0)

    blocks = rows // BLK
    links = [(i, j) for i in range(blocks) for j in range(i)]
    for x, (i, j) in enumerate(links):
        cross[x] = jnp.full((PAIR, QB), same_owner(lens_ref, j, i), jnp.int32).astype(F32).astype(BF16)

    def linked(value, qc, kc):
        i, j = qc * QB // BLK, kc * QB // BLK
        return value if i == j else value * cross[links.index((i, j))]

    for k in range(nq):
        there.finish(k)
        at = there.chunk(k)
        box = inbox[pl.ds(at * group, group)].reshape(QB, width)
        part = dot_nn(pick[:, pl.ds(pl.multiple_of(at * QB, QB), QB)], box).astype(BF16)
        if k == 0:
            tok[...] = part
        else:
            tok[...] += part

    lane = lax.broadcasted_iota(jnp.int32, (1, PAIR), 1) // head
    picks = [jnp.where(lane == h, 1.0, 0.0).astype(BF16) for h in range(two)]

    def project(c, carry):
        r = pl.ds(pl.multiple_of(c * QB, QB), QB)
        x = tok[r, :]
        for g in range(4):
            rs = slice(g * width, (g + 1) * width)
            u = dot_nt(hgrad_t[rs, :width], x)
            w = jnp.tanh(u) + 1.0
            a = u * w
            low = a.astype(BF16)
            wb = w.astype(BF16)
            slope_t[rs, r] = wb + low * (2.0 - wb)
            if g == 0:
                gate_t[:, r] = low
            elif g == 2:
                q_t[:, :, r] = (low * (0.5 * head**-0.5)).reshape(pairs, PAIR, QB)
            else:
                here, flat = (v_t, v_z) if g == 1 else (k_t, k_z)
                here[:, :, r] = low.reshape(HEADS, head, QB)
                for p in range(pairs):
                    tall = jnp.transpose(low[p * PAIR : (p + 1) * PAIR])
                    for h in range(two):
                        flat[p * two + h, r, :] = tall * picks[h]
        return carry

    lax.fori_loop(0, nq, project, 0)

    tiles = [(qc, kc) for qc in range(nq) for kc in range(qc + 1)]
    low_i = lax.broadcasted_iota(jnp.int32, (QB, QB), 0)
    high_i = lax.broadcasted_iota(jnp.int32, (QB, QB), 1)

    def span(c):
        return slice(c * QB, (c + 1) * QB)

    def forward(p, carry):
        tri = jnp.where(low_i <= high_i, 1.0, 0.0).astype(BF16)
        work = [(h, qc, kc) for h in range(two) for qc, kc in tiles]
        held = {}
        out = None
        for i in range(len(work) + LAG):
            if i < len(work):
                h, qc, kc = work[i]
                q = linked(q_t[p, :, span(qc)], qc, kc)
                held[i] = dot_nn(k_z[p * two + h, span(kc), :], q)
            if i < LAG:
                continue
            h, qc, kc = work[i - LAG]
            u = held.pop(i - LAG)
            g = p * two + h
            w = jnp.tanh(u) + 1.0
            a = (u * w).astype(BF16)
            wb = w.astype(BF16)
            s = wb + a * (2.0 - wb)
            if qc == kc:
                a = a * tri
                s = s * tri
            attn[g, tiles.index((qc, kc))] = a
            slopes[g, tiles.index((qc, kc))] = s
            o = dot_nn(v_t[g, :, span(kc)], a)
            out = o if kc == 0 else out + o
            if qc == kc:
                att_t[g, :, span(qc)] = out
        return carry

    lax.fori_loop(0, pairs, forward, 0)

    def norm(c, carry):
        r = pl.ds(pl.multiple_of(c * 128, 128), 128)
        x = att_t[:, :, r].reshape(width, 128)
        centred = x - jnp.mean(x, axis=0, keepdims=True)
        spread = jnp.mean(centred * centred, axis=0, keepdims=True)
        inv = lax.rsqrt(spread + NORM_EPS)
        unit = centred * inv
        g = gate_t[:, r].astype(F32)
        mixed_t[:, r] = (unit * g).astype(BF16)
        dm = dmix_t[:, r].astype(F32)
        hgrad_t[:width, r] = (dm * unit * slope_t[:width, r].astype(F32)).astype(BF16)
        dn = dm * g
        mean_a = jnp.mean(dn, axis=0, keepdims=True)
        mean_b = jnp.mean(dn * unit, axis=0, keepdims=True)
        dout_t[:, :, r] = (
            (inv * (dn - mean_a - unit * mean_b)).astype(BF16).reshape(pairs, PAIR, 128)
        )
        return carry

    lax.fori_loop(0, rows // 128, norm, 0)

    sources = bufs[:4]
    hops = bufs[4:]

    def hop(chain, stage):
        bit = chain_bits(bits, chain % 2 == 1)[stage]
        mine = (me // (1 << bit)) % 2
        peer = me + (1 - 2 * mine) * (1 << bit)
        cur = sources[chain] if stage == 0 else hops[chain * bits + stage - 1]
        got = hops[chain * bits + stage]
        half = cur.shape[0] // 2
        copy = pltpu.make_async_remote_copy(
            src_ref=cur.at[pl.ds((1 - mine) * half, half)],
            dst_ref=got,
            send_sem=hs.at[chain * bits + stage],
            recv_sem=hr.at[chain * bits + stage],
            device_id=(peer,),
            device_id_type=MESH,
        )
        return copy, cur.at[pl.ds(mine * half, half)], got

    half_w = width // 2
    wide = 3 * half_w
    if direct:
        columns = [
            [(0, width)],
            None,
            [(width * g, half_w) for g in (1, 2, 3)],
            [(width * g + half_w, half_w) for g in (1, 2, 3)],
        ]
    else:
        columns = [[(0, width)], None, [(width, wide)], [(width + wide, wide)]]

    def advance(chain, stage):
        copy, kept, got = hop(chain, stage)
        copy.wait()
        total = kept[...].astype(F32) + got[...].astype(F32)
        if stage < bits - 1:
            got[...] = total.astype(BF16)
            hop(chain, stage + 1)[0].start()
        elif not direct:
            sums[chain][...] = total
        elif chain == 1:
            no_ref[...] = DECAY * mo_ref[...] + scale * total
        else:
            at = 0
            for start, size in columns[chain]:
                cols = slice(start, start + size)
                ni_ref[:, cols] = DECAY * mi_ref[:, cols] + scale * total[:, at : at + size]
                at += size

    def weight_grad(chain):
        order = chain_bits(bits, chain % 2 == 1)
        if direct:
            at = 0
            for start, size in columns[chain] or [(0, width)]:
                for j in range(0, size, QB):
                    lo = start + j
                    if chain == 1:
                        part = dot_nn(mixed_t[...], og_ref[:, lo : lo + QB])
                    else:
                        part = dot_nt(tok_t[...], hgrad_t[lo : lo + QB, :])
                    part = part.astype(BF16)
                    for slot in range(n):
                        d = slot_device(slot, n, order)
                        sources[chain][slot * per : (slot + 1) * per, at : at + QB] = part[
                            d * per : (d + 1) * per
                        ]
                    at += QB
        else:
            base, size = (columns[chain] or [(0, width)])[0]
            thin = size // fold
            step = QB if thin % QB == 0 else thin
            strip = 128

            def fold_rows(x, carry):
                lo = pl.multiple_of(x * strip, strip)
                spot = pl.ds(lo, strip)
                for turn in range(fold):
                    mat = order_block(strip, lo, width, n, per, order, fold, turn)
                    if chain == 1:
                        left = dot_nn(mat, mixed_t[...]).astype(BF16)
                    else:
                        left = dot_nt(mat, tok[...]).astype(BF16)
                    for j in range(thin // step):
                        start = base + turn * thin + j * step
                        if chain == 1:
                            part = dot_nn(left, og_ref[:, start : start + step])
                        else:
                            part = dot_nt(left, hgrad_t[start : start + step, :])
                        cols = slice(j * step, (j + 1) * step)
                        if turn == 0:
                            sources[chain][spot, cols] = part.astype(BF16)
                        else:
                            sources[chain][spot, cols] += part.astype(BF16)
                return carry

            lax.fori_loop(0, n * per * fold // strip, fold_rows, 0)
        hop(chain, 0)[0].start()

    if direct:
        for c in range(nq):
            tok_t[:, span(c)] = jnp.transpose(tok[span(c), :])
    weight_grad(0)
    weight_grad(1)

    def backward(p, carry):
        work = [(h, qc, kc) for h in range(two) for kc in range(nq) for qc in range(kc, nq)]
        held = {}
        dk = dv = None
        for i in range(len(work) + LAG):
            if i < len(work):
                h, qc, kc = work[i]
                d = linked(dout_t[p, :, span(qc)], qc, kc)
                held[i] = dot_nn(v_z[p * two + h, span(kc), :], d)
            if i < LAG:
                continue
            h, qc, kc = work[i - LAG]
            u = held.pop(i - LAG)
            g = p * two + h
            t = tiles.index((qc, kc))
            hr_ = slice(h * head, (h + 1) * head)
            ds = u.astype(BF16) * slopes[g, t]
            dq = dot_nn(k_t[g, :, span(kc)], ds)
            if kc == 0:
                acc[h, :, span(qc)] = dq
            else:
                acc[h, :, span(qc)] += dq
            one = dot_nt(q_t[p, hr_, span(qc)], ds)
            two_ = dot_nt(dout_t[p, hr_, span(qc)], attn[g, t])
            dk = one if qc == kc else dk + one
            dv = two_ if qc == kc else dv + two_
            if qc == nq - 1:
                for grp, val in ((1, dv), (3, dk)):
                    rs = pl.ds(pl.multiple_of(grp * width + p * PAIR + h * head, head), head)
                    hgrad_t[rs, span(kc)] = (
                        val.astype(BF16).astype(F32) * slope_t[rs, span(kc)].astype(F32)
                    ).astype(BF16)
            if kc == qc:
                rs = pl.ds(pl.multiple_of(2 * width + p * PAIR + h * head, head), head)
                full = (acc[h, :, span(qc)] * (0.5 * head**-0.5)).astype(BF16).astype(F32)
                hgrad_t[rs, span(qc)] = (full * slope_t[rs, span(qc)].astype(F32)).astype(BF16)

        @pl.when(p == 0)
        def _():
            advance(0, 0)
            advance(1, 0)

        if direct:

            @pl.when(p == pairs // 2 - 1)
            def _():
                weight_grad(2)

        @pl.when(p == pairs - 2)
        def _():
            advance(0, 1)
            advance(1, 1)

        @pl.when(p == pairs - 1)
        def _():
            if direct:
                advance(2, 0)
            advance(0, 2)
            advance(1, 2)

        return carry

    lax.fori_loop(0, pairs, backward, 0)

    def tokens_back(c, carry):
        r = pl.ds(pl.multiple_of(c * QB, QB), QB)
        dmix_t[:, r] = (
            og_t[:, r].astype(F32) + dot_nn(w_ref[:, : 4 * width], hgrad_t[:, r])
        ).astype(BF16)
        return carry

    lax.fori_loop(0, nq, tokens_back, 0)

    for k in range(nq):
        at = back.chunk(k)
        r = pl.ds(pl.multiple_of(at * QB, QB), QB)
        part = dot_nt(place[r, :], dmix_t[...]).astype(BF16)
        outbox[pl.ds(at * group, group)] = part.reshape(group, cap, width)
        back.start(k)
    if not direct:
        weight_grad(2)
    weight_grad(3)
    inbox2[me] = outbox[me]
    gather_matrix(home_ref, pick)
    if not direct:
        advance(2, 0)
    for stage in range(bits):
        if stage >= 3:
            advance(0, stage)
            advance(1, stage)
        if stage >= 1:
            advance(2, stage)
        advance(3, stage)
    for k in range(nq):
        back.finish(k)
        at = back.chunk(k)
        box = inbox2[pl.ds(at * group, group)].reshape(QB, width)
        part = dot_nn(pick[:, pl.ds(pl.multiple_of(at * QB, QB), QB)], box).astype(BF16)
        if k == 0:
            tok[...] = part
        elif k < nq - 1:
            tok[...] += part
        else:
            out_ev[...] = tok[...] + part


def shards(n, events, home_slot, dest_slot, seq_lens, weights, out_grad, momentum_in, momentum_out):
    rows, width = events.shape
    cap = rows // n
    bits = n.bit_length() - 1
    per = width // n
    fold = max(1, 16 // per)
    tall = per * fold
    direct = fold == 1
    nq = rows // QB
    pairs = width // PAIR
    head = width // HEADS
    scale = (n * rows) ** (-0.5)
    home = home_slot.reshape(1, rows)
    dest = dest_slot.reshape(1, rows)
    vm = pl.BlockSpec(memory_space=pltpu.VMEM)
    sm = pl.BlockSpec(memory_space=pltpu.SMEM)
    hbm = pl.BlockSpec(memory_space=pl.ANY)
    dma = pltpu.SemaphoreType.DMA
    wides = (width, width, 3 * width // 2, 3 * width // 2)
    thins = [w // fold for w in wides]
    bufs = [pltpu.VMEM((n * tall, t), BF16) for t in thins]
    for t in thins:
        for stage in range(bits):
            bufs.append(pltpu.VMEM((n * tall >> (stage + 1), t), BF16))

    def area(*shape, kind=BF16):
        return pltpu.VMEM(shape, kind)

    boxed = area(n, cap, width)
    ntile = nq * (nq + 1) // 2
    blocks = rows // BLK
    ev_shape = jax.ShapeDtypeStruct(events.shape, BF16)
    if direct:
        outs = [
            ev_shape,
            jax.ShapeDtypeStruct(momentum_in.shape, F32),
            jax.ShapeDtypeStruct(momentum_out.shape, F32),
        ]
        more = (momentum_in, momentum_out)
    else:
        outs = [ev_shape] + [jax.ShapeDtypeStruct((tall, t), F32) for t in thins]
        more = ()
    got = pl.pallas_call(
        functools.partial(step_kernel, n, scale, direct),
        out_shape=outs,
        in_specs=[sm, vm, vm, vm, hbm, hbm] + [vm] * len(more),
        out_specs=[vm] * len(outs),
        scratch_shapes=[
            area(width, 5 * width),
            area(rows, width),
            area(width, rows),
            boxed,
            boxed,
            boxed,
            area(rows, rows),
            area(rows, rows),
            area(rows, width),
            area(width, rows),
            area(width, rows),
            area(4 * width, rows),
            area(width, rows),
            area(HEADS, head, rows),
            area(pairs, PAIR, rows),
            area(HEADS, head, rows),
            area(HEADS, rows, PAIR),
            area(HEADS, rows, PAIR),
            area(HEADS, ntile, QB, QB),
            area(HEADS, ntile, QB, QB),
            area(HEADS, head, rows, kind=F32),
            area(4 * width, rows),
            area(width, rows),
            area(pairs, PAIR, rows),
            area(PAIR // head, head, rows, kind=F32),
            area(max(1, blocks * (blocks - 1) // 2), PAIR, QB),
            dma((2,)),
            dma((n,)),
            dma((n,)),
            dma((n,)),
            dma((n,)),
            dma((4 * bits,)),
            dma((4 * bits,)),
        ]
        + bufs,
        compiler_params=pltpu.CompilerParams(
            collective_id=0, has_side_effects=True, vmem_limit_bytes=VMEM_LIMIT
        ),
        name="step",
    )(seq_lens, home, dest, events, weights, out_grad, *more)
    if direct:
        return tuple(got)
    ev, *parts = got
    f0, f1, f2, f3 = [
        f.reshape(fold, per, f.shape[1]).transpose(1, 0, 2).reshape(per, fold * f.shape[1])
        for f in parts
    ]
    return (
        ev,
        DECAY * momentum_in + scale * jnp.concatenate([f0, f2, f3], axis=1),
        DECAY * momentum_out + scale * f1,
    )


def solution(mesh):
    n = mesh.shape["dp"]
    row = P("dp", None)
    return jax.shard_map(
        functools.partial(shards, n),
        mesh=mesh,
        in_specs=(row, P("dp"), P("dp"), P("dp"), P(), row, row, row),
        out_specs=(row, row, row),
        check_vma=False,
    )
```

```python
import functools

import jax
import jax.numpy as jnp
from jax import lax
from jax.experimental import pallas as pl
from jax.experimental.pallas import tpu as pltpu
from jax.sharding import PartitionSpec as P

HEADS = 8
BLK = 512
QB = 256
PAIR = 128
NORM_EPS = 1e-05
DECAY = 0.9
MESH = pl.DeviceIdType.MESH
F32 = jnp.float32
BF16 = jnp.bfloat16
VMEM_LIMIT = 67 * 1000 * 1000
LAG = 2
LATE = ((4, 0), (3, 1), (2, 2), (4, 1), (0, 4), (1, 4), (3, 2), (2, 3), (4, 2), (3, 3), (2, 4), (4, 3), (3, 4), (4, 4))
PLAN = (('fill', 3), ('fill', 1), ('msg', 3, 0), ('msg', 1, 0), ('msg', 3, 1), ('msg', 1, 1), ('msg', 3, 2), ('msg', 1, 2), ('msg', 3, 3), ('msg', 1, 3), ('fill', 2), ('fill', 0), ('own',), ('msg', 3, 4), ('msg', 1, 4), ('msg', 3, 5), ('msg', 1, 5), ('grad', 4), ('gone', 3, 0), ('gone', 1, 0), ('msg', 3, 6), ('msg', 1, 6), ('add', 3, 1), ('add', 2, 2), ('gone', 3, 1), ('gone', 1, 1), ('msg', 3, 7), ('msg', 1, 7), ('add', 4, 0), ('gone', 3, 2), ('gone', 1, 2), ('msg', 2, 0), ('msg', 0, 1), ('add', 0, 4), ('add', 1, 4), ('gone', 3, 3), ('gone', 1, 3), ('msg', 2, 1), ('msg', 0, 2), ('add', 4, 1), ('add', 3, 2), ('gone', 3, 4), ('gone', 1, 4), ('msg', 2, 2), ('msg', 0, 3), ('add', 2, 3), ('gone', 3, 5), ('gone', 1, 5), ('msg', 2, 3), ('msg', 0, 4), ('add', 4, 2), ('add', 3, 3), ('gone', 3, 6), ('gone', 1, 6), ('msg', 2, 4), ('msg', 0, 5), ('gone', 3, 7), ('gone', 1, 7), ('msg', 2, 5), ('msg', 0, 6), ('add', 2, 4), ('add', 4, 3), ('add', 3, 4), ('gone', 2, 0), ('gone', 0, 1), ('msg', 2, 6), ('msg', 0, 7), ('gone', 2, 1), ('gone', 0, 2), ('msg', 2, 7), ('add', 4, 4), ('pick',), ('get', 0), ('get', 1), ('get', 2), ('get', 3), ('gone', 2, 2), ('gone', 0, 3), ('gone', 2, 3), ('gone', 0, 4), ('gone', 2, 4), ('gone', 0, 5), ('gone', 2, 5), ('gone', 0, 6), ('gone', 2, 6), ('gone', 0, 7), ('gone', 2, 7))
WHOLE_PLAN = (
    *((what, k) for k in range(4) for what in ("fill", "start")),
    ("grad", 2),
    ("grad", 3),
    ("pick",),
    *(("add", chain, stage) for stage in (3, 4, 5, 6) for chain in (0, 1)),
    *(("add", chain, stage) for stage in range(7) for chain in (2, 3)),
    ("own",),
    *(("get", k) for k in range(4)),
    *(("sent", k) for k in range(4)),
)


def dot_nn(a, b):
    return lax.dot_general(a, b, (((1,), (0,)), ((), ())), preferred_element_type=F32)


def dot_nt(a, b):
    return lax.dot_general(a, b, (((1,), (1,)), ((), ())), preferred_element_type=F32)


def chain_bits(bit_count, second):
    order = list(range(bit_count))
    if second and bit_count > 2:
        order[1], order[2] = order[2], order[1]
    return order


def slot_device(slot, n, bits):
    return sum(((slot // (n >> (rank + 1))) % 2) << bit for rank, bit in enumerate(bits))


def enter_all(n, me):
    barrier = pltpu.get_barrier_semaphore()

    def greet(i, carry):
        pl.semaphore_signal(barrier, inc=1, device_id=((me + i) % n,), device_id_type=MESH)
        return carry

    lax.fori_loop(1, n, greet, 0)
    return barrier


def flip(value, other, size):
    total = 0
    weight = 1
    while weight < size:
        total = total + (value // weight + other // weight) % 2 * weight
        weight *= 2
    return total


class Exchange:
    def __init__(self, n, me, group, src, dst, ssem, rsem):
        self.n, self.me, self.group = n, me, group
        self.src, self.dst, self.ssem, self.rsem = src, dst, ssem, rsem

    def chunk(self, k):
        return flip(self.me // self.group, k, self.n // self.group)

    def copy(self, k, j):
        peer = self.chunk(k) * self.group + flip(self.me % self.group, j, self.group)
        i = k * self.group + j
        return pltpu.make_async_remote_copy(
            src_ref=self.src.at[peer],
            dst_ref=self.dst.at[self.me],
            send_sem=self.ssem.at[i],
            recv_sem=self.rsem.at[i],
            device_id=(peer,),
            device_id_type=MESH,
        )

    def each(self, k, act):
        def go(j, carry):
            act(self.copy(k, j))
            return carry

        lax.fori_loop(1 if k == 0 else 0, self.group, go, 0)

    def start(self, k):
        self.each(k, lambda copy: copy.start())

    def sent(self, k):
        self.each(k, lambda copy: copy.wait_send())

    def arrived(self, k):
        self.each(k, lambda copy: copy.wait_recv())

    def finish(self, k):
        self.each(k, lambda copy: copy.wait())


def gather_matrix(slots_ref, out_ref):
    rows = out_ref.shape[0]
    wide = jnp.broadcast_to(slots_ref[...].astype(F32), (128, rows))
    column = jnp.transpose(wide)
    lane = lax.broadcasted_iota(jnp.int32, (rows, 128), 1).astype(F32)
    for j in range(rows // 128):
        out_ref[:, j * 128 : (j + 1) * 128] = jnp.where(
            column == lane + float(j * 128), 1.0, 0.0
        ).astype(BF16)


def scatter_chunk(slots_ref, start, size):
    rows = slots_ref.shape[1]
    place = lax.broadcasted_iota(jnp.int32, (size, rows), 0) + start
    return jnp.where(place == slots_ref[...], 1.0, 0.0).astype(BF16)


def same_owner(lens_ref, low, high):
    start = 0
    same = 0
    for j in range(lens_ref.shape[0]):
        blocks = (lens_ref[j] + BLK - 1) // BLK
        inside = jnp.where((start <= low) & (high < start + blocks), 1, 0)
        same = same + inside
        start = start + blocks
    return same


def order_block(height, base, width, n, per, bits, fold, turn):
    shape = (height, width)
    tall = per * fold
    place = lax.broadcasted_iota(jnp.int32, shape, 0) + base
    column = lax.broadcasted_iota(jnp.int32, shape, 1)
    slot = place // tall
    rest = place % tall
    device = jnp.zeros(shape, jnp.int32)
    for rank, bit in enumerate(bits):
        weight = n >> (rank + 1)
        device = device + ((slot // weight) % 2) * (1 << bit)
    hit = (column == device * per + rest % per) & (rest // per == turn)
    return jnp.where(hit, 1.0, 0.0).astype(BF16)


def step_kernel(n, direct, lens_hbm, home_hbm, dest_hbm, ev_hbm, w_hbm, og_hbm, *refs):
    chains = 5 if direct else 4
    out_ev, sums, refs = refs[0], refs[1 : 1 + chains], refs[1 + chains :]
    (
        lens_ref, home_ref, dest_ref, ev_ref,
        w_ref, og_ref, og_t, outbox, inbox, inbox2, pick, place, tok, tok_t, dmix_t,
        slope_t, gate_t, v_t, q_t, k_t, k_z, v_z, attn, slopes, att_t, hgrad_t, mixed_t,
        dout_t, acc, cross, lsem, ssem, rsem, ssem2, rsem2, hs, hr, *bufs,
    ) = refs
    me = lax.axis_index("dp")
    rows, width = ev_ref.shape
    cap = rows // n
    per = width // n
    fold = max(1, 16 // per)
    nq = rows // QB
    bits = n.bit_length() - 1
    group = QB // cap
    head = width // HEADS
    pairs = width // PAIR
    two = PAIR // head
    barrier = enter_all(n, me)
    loads = [
        pltpu.make_async_copy(src, dst, lsem.at[i])
        for i, (src, dst) in enumerate(
            (
                (home_hbm, home_ref),
                (ev_hbm, ev_ref),
                (dest_hbm, dest_ref),
                (og_hbm, og_ref),
                (w_hbm, w_ref),
                (lens_hbm, lens_ref),
            )
        )
    ]
    for load in loads:
        load.start()
    loads[0].wait()
    loads[1].wait()
    there = Exchange(n, me, group, outbox, inbox, ssem, rsem)
    back = Exchange(n, me, group, outbox, inbox2, ssem2, rsem2)

    for k in range(nq):
        at = there.chunk(k)
        part = dot_nn(scatter_chunk(home_ref, at * QB, QB), ev_ref[...]).astype(BF16)
        outbox[pl.ds(at * group, group)] = part.reshape(group, cap, width)
        if k == 0:
            pl.semaphore_wait(barrier, n - 1)
        there.start(k)
    inbox[me] = outbox[me]
    for load in loads[2:]:
        load.wait()
    gather_matrix(dest_ref, pick)

    def prepare(c, carry):
        r = pl.ds(pl.multiple_of(c * QB, QB), QB)
        place[r, :] = scatter_chunk(dest_ref, c * QB, QB)
        x = og_ref[r, :]
        og_t[:, r] = jnp.transpose(x)
        dmix_t[:, r] = (dot_nt(w_ref[:, 4 * width :], x) * 0.5).astype(BF16)
        return carry

    lax.fori_loop(0, nq, prepare, 0)

    def turn_w(c, carry):
        r = pl.ds(pl.multiple_of(c * QB, QB), QB)
        hgrad_t[r, :width] = jnp.transpose(w_ref[:, r]) * 0.5
        return carry

    lax.fori_loop(0, 4 * width // QB, turn_w, 0)

    blocks = rows // BLK
    links = [(i, j) for i in range(blocks) for j in range(i)]
    for x, (i, j) in enumerate(links):
        cross[x] = jnp.full((PAIR, QB), same_owner(lens_ref, j, i), jnp.int32).astype(F32).astype(BF16)

    def linked(value, qc, kc):
        i, j = qc * QB // BLK, kc * QB // BLK
        return value if i == j else value * cross[links.index((i, j))]

    for k in range(nq):
        there.finish(k)
        at = there.chunk(k)
        box = inbox[pl.ds(at * group, group)].reshape(QB, width)
        part = dot_nn(pick[:, pl.ds(pl.multiple_of(at * QB, QB), QB)], box).astype(BF16)
        if k == 0:
            tok[...] = part
        else:
            tok[...] += part

    lane = lax.broadcasted_iota(jnp.int32, (1, PAIR), 1) // head
    picks = [jnp.where(lane == h, 1.0, 0.0).astype(BF16) for h in range(two)]

    def project(c, carry):
        r = pl.ds(pl.multiple_of(c * QB, QB), QB)
        x = tok[r, :]
        for g in range(4):
            rs = slice(g * width, (g + 1) * width)
            u = dot_nt(hgrad_t[rs, :width], x)
            w = jnp.tanh(u) + 1.0
            a = u * w
            low = a.astype(BF16)
            wb = w.astype(BF16)
            slope_t[rs, r] = wb + low * (2.0 - wb)
            if g == 0:
                gate_t[:, r] = low
            elif g == 2:
                q_t[:, :, r] = (low * (0.5 * head**-0.5)).reshape(pairs, PAIR, QB)
            else:
                here, flat = (v_t, v_z) if g == 1 else (k_t, k_z)
                here[:, :, r] = low.reshape(HEADS, head, QB)
                for p in range(pairs):
                    tall = jnp.transpose(low[p * PAIR : (p + 1) * PAIR])
                    for h in range(two):
                        flat[p * two + h, r, :] = tall * picks[h]
        return carry

    lax.fori_loop(0, nq, project, 0)

    tiles = [(qc, kc) for qc in range(nq) for kc in range(qc + 1)]
    low_i = lax.broadcasted_iota(jnp.int32, (QB, QB), 0)
    high_i = lax.broadcasted_iota(jnp.int32, (QB, QB), 1)

    def span(c):
        return slice(c * QB, (c + 1) * QB)

    def forward(p, carry):
        tri = jnp.where(low_i <= high_i, 1.0, 0.0).astype(BF16)
        work = [(h, qc, kc) for h in range(two) for qc, kc in tiles]
        held = {}
        out = None
        for i in range(len(work) + LAG):
            if i < len(work):
                h, qc, kc = work[i]
                q = linked(q_t[p, :, span(qc)], qc, kc)
                held[i] = dot_nn(k_z[p * two + h, span(kc), :], q)
            if i < LAG:
                continue
            h, qc, kc = work[i - LAG]
            u = held.pop(i - LAG)
            g = p * two + h
            w = jnp.tanh(u) + 1.0
            a = (u * w).astype(BF16)
            wb = w.astype(BF16)
            if qc == kc:
                a = a * tri
                wb = wb * tri
            attn[g, tiles.index((qc, kc))] = a
            slopes[g, tiles.index((qc, kc))] = wb
            o = dot_nn(v_t[g, :, span(kc)], a)
            out = o if kc == 0 else out + o
            if qc == kc:
                att_t[g, :, span(qc)] = out
        return carry

    lax.fori_loop(0, pairs, forward, 0)

    def norm(c, carry):
        r = pl.ds(pl.multiple_of(c * 128, 128), 128)
        x = att_t[:, :, r].reshape(width, 128)
        centred = x - jnp.mean(x, axis=0, keepdims=True)
        spread = jnp.mean(centred * centred, axis=0, keepdims=True)
        inv = lax.rsqrt(spread + NORM_EPS)
        unit = centred * inv
        g = gate_t[:, r].astype(F32)
        mixed_t[:, r] = (unit * g).astype(BF16)
        dm = dmix_t[:, r].astype(F32)
        hgrad_t[:width, r] = (dm * unit * slope_t[:width, r].astype(F32)).astype(BF16)
        dn = dm * g
        mean_a = jnp.mean(dn, axis=0, keepdims=True)
        mean_b = jnp.mean(dn * unit, axis=0, keepdims=True)
        dout_t[:, :, r] = (
            (inv * (dn - mean_a - unit * mean_b)).astype(BF16).reshape(pairs, PAIR, 128)
        )
        return carry

    lax.fori_loop(0, rows // 128, norm, 0)

    sources = bufs[:chains]
    hops = bufs[chains:]
    orders = [chain_bits(bits, chain in (1, 2)) for chain in range(chains)]

    def hop(chain, stage):
        bit = orders[chain][stage]
        mine = (me // (1 << bit)) % 2
        peer = me + (1 - 2 * mine) * (1 << bit)
        cur = sources[chain] if stage == 0 else hops[chain * bits + stage - 1]
        got = hops[chain * bits + stage]
        half = cur.shape[0] // 2
        copy = pltpu.make_async_remote_copy(
            src_ref=cur.at[pl.ds((1 - mine) * half, half)],
            dst_ref=got,
            send_sem=hs.at[chain * bits + stage],
            recv_sem=hr.at[chain * bits + stage],
            device_id=(peer,),
            device_id_type=MESH,
        )
        return copy, cur.at[pl.ds(mine * half, half)], got

    columns = chain_columns(width, direct)

    def advance(chain, stage):
        copy, kept, got = hop(chain, stage)
        copy.wait()
        total = kept[...].astype(F32) + got[...].astype(F32)
        if stage == bits - 1:
            sums[chain][...] = total
        else:
            got[...] = total.astype(BF16)
            hop(chain, stage + 1)[0].start()

    def weight_grad(chain):
        order = orders[chain]
        if direct:
            pieces = [
                (start + j, PAIR) for start, size in columns[chain] for j in range(0, size, PAIR)
            ]
            for x in range(0, len(pieces), 2):
                some = pieces[x : x + 2]
                if chain == 1:
                    right = [og_ref[:, lo : lo + size] for lo, size in some]
                    part = dot_nn(mixed_t[...], jnp.concatenate(right, axis=1))
                else:
                    right = [hgrad_t[lo : lo + size, :] for lo, size in some]
                    part = dot_nt(tok_t[...], jnp.concatenate(right, axis=0))
                part = part.astype(BF16)
                cols = slice(x * PAIR, x * PAIR + part.shape[1])
                for slot in range(n):
                    d = slot_device(slot, n, order)
                    sources[chain][slot * per : (slot + 1) * per, cols] = part[d * per : (d + 1) * per]
        else:
            base, size = columns[chain][0]
            thin = size // fold
            step = QB if thin % QB == 0 else thin
            strip = 128

            def fold_rows(x, carry):
                lo = pl.multiple_of(x * strip, strip)
                spot = pl.ds(lo, strip)
                for turn in range(fold):
                    mat = order_block(strip, lo, width, n, per, order, fold, turn)
                    if chain == 1:
                        left = dot_nn(mat, mixed_t[...]).astype(BF16)
                    else:
                        left = dot_nt(mat, tok[...]).astype(BF16)
                    for j in range(thin // step):
                        start = base + turn * thin + j * step
                        if chain == 1:
                            part = dot_nn(left, og_ref[:, start : start + step])
                        else:
                            part = dot_nt(left, hgrad_t[start : start + step, :])
                        cols = slice(j * step, (j + 1) * step)
                        if turn == 0:
                            sources[chain][spot, cols] = part.astype(BF16)
                        else:
                            sources[chain][spot, cols] += part.astype(BF16)
                return carry

            lax.fori_loop(0, n * per * fold // strip, fold_rows, 0)
        hop(chain, 0)[0].start()

    if direct:
        for c in range(nq):
            tok_t[:, span(c)] = jnp.transpose(tok[span(c), :])
    weight_grad(0)
    weight_grad(1)

    def backward(p, carry):
        work = [(h, qc, kc) for h in range(two) for kc in range(nq) for qc in range(kc, nq)]
        held = {}
        dk = dv = None
        for i in range(len(work) + LAG):
            if i < len(work):
                h, qc, kc = work[i]
                d = linked(dout_t[p, :, span(qc)], qc, kc)
                held[i] = dot_nn(v_z[p * two + h, span(kc), :], d)
            if i < LAG:
                continue
            h, qc, kc = work[i - LAG]
            u = held.pop(i - LAG)
            g = p * two + h
            t = tiles.index((qc, kc))
            hr_ = slice(h * head, (h + 1) * head)
            a = attn[g, t]
            wb = slopes[g, t]
            ds = u.astype(BF16) * (wb + a * (2.0 - wb))
            dq = dot_nn(k_t[g, :, span(kc)], ds)
            if kc == 0:
                acc[h, :, span(qc)] = dq
            else:
                acc[h, :, span(qc)] += dq
            one = dot_nt(q_t[p, hr_, span(qc)], ds)
            two_ = dot_nt(dout_t[p, hr_, span(qc)], a)
            dk = one if qc == kc else dk + one
            dv = two_ if qc == kc else dv + two_
            if qc == nq - 1:
                for grp, val in ((1, dv), (3, dk)):
                    rs = pl.ds(pl.multiple_of(grp * width + p * PAIR + h * head, head), head)
                    hgrad_t[rs, span(kc)] = (
                        val.astype(BF16).astype(F32) * slope_t[rs, span(kc)].astype(F32)
                    ).astype(BF16)
            if kc == qc:
                rs = pl.ds(pl.multiple_of(2 * width + p * PAIR + h * head, head), head)
                full = (acc[h, :, span(qc)] * (0.5 * head**-0.5)).astype(BF16).astype(F32)
                hgrad_t[rs, span(qc)] = (full * slope_t[rs, span(qc)].astype(F32)).astype(BF16)

        @pl.when(p == 0)
        def _():
            advance(0, 0)
            advance(1, 0)

        if direct:

            @pl.when(p == pairs - 3)
            def _():
                weight_grad(2)

        @pl.when(p == pairs - 2)
        def _():
            advance(0, 1)
            advance(1, 1)
            if direct:
                advance(2, 0)
                weight_grad(3)

        @pl.when(p == pairs - 1)
        def _():
            advance(0, 2)
            advance(1, 2)
            if direct:
                advance(3, 0)

        return carry

    lax.fori_loop(0, pairs, backward, 0)

    def tokens_back(c, carry):
        r = pl.ds(pl.multiple_of(c * QB, QB), QB)
        dmix_t[:, r] = (
            og_t[:, r].astype(F32) + dot_nn(w_ref[:, : 4 * width], hgrad_t[:, r])
        ).astype(BF16)
        return carry

    lax.fori_loop(0, nq, tokens_back, 0)

    if direct:
        advance(2, 1)
        advance(0, 3)
        advance(1, 3)
    def fill_back(k):
        at = back.chunk(k)
        r = pl.ds(pl.multiple_of(at * QB, QB), QB)
        part = dot_nt(place[r, :], dmix_t[...]).astype(BF16)
        outbox[pl.ds(at * group, group)] = part.reshape(group, cap, width)

    def collect(k):
        back.arrived(k)
        at = back.chunk(k)
        box = inbox2[pl.ds(at * group, group)].reshape(QB, width)
        part = dot_nn(pick[:, pl.ds(pl.multiple_of(at * QB, QB), QB)], box).astype(BF16)
        if k == 0:
            tok[...] = part
        else:
            tok[...] += part

    plan = PLAN if direct else WHOLE_PLAN
    for what, *args in plan:
        if what == "fill":
            fill_back(*args)
        elif what == "start":
            back.start(*args)
        elif what == "sent":
            back.sent(*args)
        elif what == "msg":
            back.copy(*args).start()
        elif what == "gone":
            back.copy(*args).wait_send()
        elif what == "get":
            collect(*args)
        elif what == "own":
            inbox2[me] = outbox[me]
        elif what == "grad":
            weight_grad(*args)
        elif what == "pick":
            gather_matrix(home_ref, pick)
        else:
            advance(*args)
    inbox2[me] = outbox[me]
    store = pltpu.make_async_copy(tok, out_ev, lsem.at[0])
    store.start()
    store.wait()


def chain_columns(width, direct):
    half = width // 2
    if not direct:
        return [[(0, width)], [(0, width)], [(width, 3 * half)], [(width + 3 * half, 3 * half)]]
    parts = ((0, half), (half, PAIR), (half + PAIR, PAIR))
    late = [[(width * g + at, size) for g in (1, 2, 3)] for at, size in parts]
    return [[(0, width)], [(0, width)], *late]


def finish_kernel(scale, columns, count, *refs):
    wide, spots, scratch = refs[: count + 3], refs[count + 3 : count + 6], refs[count + 6 :]
    ev_hbm, *small = wide
    held, *near, ni_ref, no_ref, isem, osem, psem = scratch
    loads, stores = [], []
    parts = osem.shape[0] - 2
    size = held.shape[0] // parts
    for i in range(parts):
        r = pl.ds(i * size, size)
        loads.append(pltpu.make_async_copy(ev_hbm.at[r], held.at[r], isem.at[i]))
        stores.append(pltpu.make_async_copy(held.at[r], spots[0].at[r], osem.at[i]))
    other = [
        pltpu.make_async_copy(src, dst, psem.at[i]) for i, (src, dst) in enumerate(zip(small, near))
    ]
    for load in [*other, *loads]:
        load.start()
    for load in other:
        load.wait()
    *sums, mi_ref, mo_ref = near
    no_ref[...] = DECAY * mo_ref[...] + scale * sums[1][...]
    for chain in range(count):
        if chain == 1:
            continue
        at = 0
        for start, span in columns[chain]:
            cols = slice(start, start + span)
            ni_ref[:, cols] = DECAY * mi_ref[:, cols] + scale * sums[chain][:, at : at + span]
            at += span
    stores.append(pltpu.make_async_copy(ni_ref, spots[1], osem.at[parts]))
    stores.append(pltpu.make_async_copy(no_ref, spots[2], osem.at[parts + 1]))
    stores[-1].start()
    stores[-2].start()
    for load, store in zip(loads, stores):
        load.wait()
        store.start()
    for store in stores:
        store.wait()


def shards(n, events, home_slot, dest_slot, seq_lens, weights, out_grad, momentum_in, momentum_out):
    rows, width = events.shape
    cap = rows // n
    bits = n.bit_length() - 1
    per = width // n
    fold = max(1, 16 // per)
    tall = per * fold
    direct = fold == 1
    nq = rows // QB
    pairs = width // PAIR
    head = width // HEADS
    scale = (n * rows) ** (-0.5)
    home = home_slot.reshape(1, rows)
    dest = dest_slot.reshape(1, rows)
    vm = pl.BlockSpec(memory_space=pltpu.VMEM)
    sm = pl.BlockSpec(memory_space=pltpu.SMEM)
    hbm = pl.BlockSpec(memory_space=pl.ANY)
    dma = pltpu.SemaphoreType.DMA
    columns = chain_columns(width, direct)
    wides = [sum(size for _, size in cols) for cols in columns]
    thins = [w // fold for w in wides]
    bufs = [pltpu.VMEM((n * tall, t), BF16) for t in thins]
    for t in thins:
        for stage in range(bits):
            bufs.append(pltpu.VMEM((n * tall >> (stage + 1), t), BF16))

    def area(*shape, kind=BF16):
        return pltpu.VMEM(shape, kind)

    boxed = area(n, cap, width)
    ntile = nq * (nq + 1) // 2
    blocks = rows // BLK
    ev_shape = jax.ShapeDtypeStruct(events.shape, BF16)
    ev, *parts = pl.pallas_call(
        functools.partial(step_kernel, n, direct),
        out_shape=[ev_shape] + [jax.ShapeDtypeStruct((tall, t), F32) for t in thins],
        in_specs=[hbm] * 6,
        out_specs=[hbm] + [vm] * len(thins),
        scratch_shapes=[
            pltpu.SMEM(seq_lens.shape, jnp.int32),
            area(1, rows, kind=jnp.int32),
            area(1, rows, kind=jnp.int32),
            area(rows, width),
            area(width, 5 * width),
            area(rows, width),
            area(width, rows),
            boxed,
            boxed,
            boxed,
            area(rows, rows),
            area(rows, rows),
            area(rows, width),
            area(width, rows),
            area(width, rows),
            area(4 * width, rows),
            area(width, rows),
            area(HEADS, head, rows),
            area(pairs, PAIR, rows),
            area(HEADS, head, rows),
            area(HEADS, rows, PAIR),
            area(HEADS, rows, PAIR),
            area(HEADS, ntile, QB, QB),
            area(HEADS, ntile, QB, QB),
            area(HEADS, head, rows, kind=F32),
            area(4 * width, rows),
            area(width, rows),
            area(pairs, PAIR, rows),
            area(PAIR // head, head, rows, kind=F32),
            area(max(1, blocks * (blocks - 1) // 2), PAIR, QB),
            dma((6,)),
            dma((n,)),
            dma((n,)),
            dma((n,)),
            dma((n,)),
            dma((len(thins) * bits,)),
            dma((len(thins) * bits,)),
        ]
        + bufs,
        compiler_params=pltpu.CompilerParams(
            collective_id=0, has_side_effects=True, vmem_limit_bytes=VMEM_LIMIT
        ),
        name="step",
    )(seq_lens, home, dest, events, weights, out_grad)
    if not direct:
        parts = [
            f.reshape(fold, per, f.shape[1]).transpose(1, 0, 2).reshape(per, fold * f.shape[1])
            for f in parts
        ]
    small = (*parts, momentum_in, momentum_out)
    return pl.pallas_call(
        functools.partial(finish_kernel, scale, columns, len(parts)),
        out_shape=[
            ev_shape,
            jax.ShapeDtypeStruct(momentum_in.shape, F32),
            jax.ShapeDtypeStruct(momentum_out.shape, F32),
        ],
        in_specs=[hbm] * (len(small) + 1),
        out_specs=[hbm] * 3,
        scratch_shapes=[
            area(rows, width),
            *(area(*x.shape, kind=F32) for x in small),
            area(*momentum_in.shape, kind=F32),
            area(*momentum_out.shape, kind=F32),
            dma((4,)),
            dma((6,)),
            dma((len(small),)),
        ],
        compiler_params=pltpu.CompilerParams(vmem_limit_bytes=VMEM_LIMIT),
        name="finish",
    )(ev, *small)


def solution(mesh):
    n = mesh.shape["dp"]
    row = P("dp", None)
    return jax.shard_map(
        functools.partial(shards, n),
        mesh=mesh,
        in_specs=(row, P("dp"), P("dp"), P("dp"), P(), row, row, row),
        out_specs=(row, row, row),
        check_vma=False,
    )
```

```python
import functools

import jax
import jax.numpy as jnp
from jax import lax
from jax.experimental import pallas as pl
from jax.experimental.pallas import tpu as pltpu
from jax.sharding import PartitionSpec as P

HEADS = 8
BLK = 512
QB = 256
PAIR = 128
NORM_EPS = 1e-05
DECAY = 0.9
MESH = pl.DeviceIdType.MESH
F32 = jnp.float32
BF16 = jnp.bfloat16
VMEM_LIMIT = 67 * 1000 * 1000
LAG = 4
BACK_LAG = 2
DEEP = 1
LATE = ((4, 0), (3, 1), (2, 2), (4, 1), (0, 4), (1, 4), (3, 2), (2, 3), (4, 2), (3, 3), (2, 4), (4, 3), (3, 4), (4, 4))
PLAN = (('fill', 3), ('fill', 1), ('msg', 3, 0), ('msg', 1, 0), ('msg', 3, 1), ('msg', 1, 1), ('msg', 3, 2), ('msg', 1, 2), ('msg', 3, 3), ('msg', 1, 3), ('fill', 0), ('fill', 2), ('own',), ('msg', 3, 4), ('msg', 1, 4), ('msg', 3, 5), ('msg', 1, 5), ('grad', 4), ('gone', 3, 0), ('gone', 1, 0), ('msg', 3, 6), ('msg', 1, 6), ('add', 2, 1), ('add', 3, 1), ('gone', 3, 1), ('gone', 1, 1), ('msg', 3, 7), ('msg', 1, 7), ('add', 4, 0), ('gone', 3, 2), ('gone', 1, 2), ('msg', 2, 0), ('msg', 0, 1), ('add', 0, 4), ('add', 1, 4), ('gone', 3, 3), ('gone', 1, 3), ('msg', 2, 1), ('msg', 0, 2), ('pick',), ('add', 2, 2), ('add', 4, 1), ('add', 3, 2), ('gone', 3, 4), ('gone', 1, 4), ('msg', 2, 2), ('msg', 0, 3), ('add', 2, 3), ('gone', 3, 5), ('gone', 1, 5), ('msg', 2, 3), ('msg', 0, 4), ('add', 4, 2), ('add', 3, 3), ('gone', 3, 6), ('gone', 1, 6), ('msg', 2, 4), ('msg', 0, 5), ('gone', 3, 7), ('gone', 1, 7), ('msg', 2, 5), ('msg', 0, 6), ('get', 1, True), ('add', 2, 4), ('add', 4, 3), ('add', 3, 4), ('gone', 2, 0), ('gone', 0, 1), ('msg', 2, 6), ('msg', 0, 7), ('gone', 2, 1), ('gone', 0, 2), ('msg', 2, 7), ('get', 0), ('get', 3), ('add', 4, 4), ('get', 2, False, True), ('gone', 2, 2), ('gone', 0, 3), ('gone', 2, 3), ('gone', 0, 4), ('gone', 2, 4), ('gone', 0, 5), ('gone', 2, 5), ('gone', 0, 6), ('gone', 2, 6), ('gone', 0, 7), ('gone', 2, 7))
WHOLE_PLAN = (
    *((what, k) for k in range(4) for what in ("fill", "start")),
    ("grad", 2),
    ("grad", 3),
    ("pick",),
    *(("add", chain, stage) for stage in (3, 4, 5, 6) for chain in (0, 1)),
    *(("add", chain, stage) for stage in range(7) for chain in (2, 3)),
    ("own",),
    ("get", 0, True),
    ("get", 1),
    ("get", 2),
    ("get", 3, False, True),
    *(("sent", k) for k in range(4)),
)


def dot_nn(a, b):
    return lax.dot_general(a, b, (((1,), (0,)), ((), ())), preferred_element_type=F32)


def dot_nt(a, b):
    return lax.dot_general(a, b, (((1,), (1,)), ((), ())), preferred_element_type=F32)


def chain_bits(bit_count, second):
    order = list(range(bit_count))
    if second and bit_count > 2:
        order[1], order[2] = order[2], order[1]
    return order


def slot_device(slot, n, bits):
    return sum(((slot // (n >> (rank + 1))) % 2) << bit for rank, bit in enumerate(bits))


def enter_all(n, me):
    barrier = pltpu.get_barrier_semaphore()

    def greet(i, carry):
        pl.semaphore_signal(barrier, inc=1, device_id=((me + i) % n,), device_id_type=MESH)
        return carry

    lax.fori_loop(1, n, greet, 0)
    return barrier


def flip(value, other, size):
    total = 0
    weight = 1
    while weight < size:
        total = total + (value // weight + other // weight) % 2 * weight
        weight *= 2
    return total


class Exchange:
    def __init__(self, n, me, group, src, dst, ssem, rsem):
        self.n, self.me, self.group = n, me, group
        self.src, self.dst, self.ssem, self.rsem = src, dst, ssem, rsem

    def chunk(self, k):
        return flip(self.me // self.group, k, self.n // self.group)

    def copy(self, k, j):
        peer = self.chunk(k) * self.group + flip(self.me % self.group, j, self.group)
        i = k * self.group + j
        return pltpu.make_async_remote_copy(
            src_ref=self.src.at[peer],
            dst_ref=self.dst.at[self.me],
            send_sem=self.ssem.at[i],
            recv_sem=self.rsem.at[i],
            device_id=(peer,),
            device_id_type=MESH,
        )

    def each(self, k, act):
        def go(j, carry):
            act(self.copy(k, j))
            return carry

        lax.fori_loop(1 if k == 0 else 0, self.group, go, 0)

    def start(self, k):
        self.each(k, lambda copy: copy.start())

    def sent(self, k):
        self.each(k, lambda copy: copy.wait_send())

    def arrived(self, k):
        self.each(k, lambda copy: copy.wait_recv())

    def finish(self, k):
        self.each(k, lambda copy: copy.wait())


def gather_matrix(slots_ref, out_ref):
    rows = out_ref.shape[0]
    wide = jnp.broadcast_to(slots_ref[...].astype(F32), (128, rows))
    column = jnp.transpose(wide)
    lane = lax.broadcasted_iota(jnp.int32, (rows, 128), 1).astype(F32)
    for j in range(rows // 128):
        out_ref[:, j * 128 : (j + 1) * 128] = jnp.where(
            column == lane + float(j * 128), 1.0, 0.0
        ).astype(BF16)


def scatter_chunk(slots_ref, start, size):
    rows = slots_ref.shape[1]
    place = lax.broadcasted_iota(jnp.int32, (size, rows), 0) + start
    return jnp.where(place == slots_ref[...], 1.0, 0.0).astype(BF16)


def same_owner(lens_ref, low, high):
    start = 0
    same = 0
    for j in range(lens_ref.shape[0]):
        blocks = (lens_ref[j] + BLK - 1) // BLK
        inside = jnp.where((start <= low) & (high < start + blocks), 1, 0)
        same = same + inside
        start = start + blocks
    return same


def order_block(height, base, width, n, per, bits, fold, turn):
    shape = (height, width)
    tall = per * fold
    place = lax.broadcasted_iota(jnp.int32, shape, 0) + base
    column = lax.broadcasted_iota(jnp.int32, shape, 1)
    slot = place // tall
    rest = place % tall
    device = jnp.zeros(shape, jnp.int32)
    for rank, bit in enumerate(bits):
        weight = n >> (rank + 1)
        device = device + ((slot // weight) % 2) * (1 << bit)
    hit = (column == device * per + rest % per) & (rest // per == turn)
    return jnp.where(hit, 1.0, 0.0).astype(BF16)


def step_kernel(n, direct, lens_hbm, home_hbm, dest_hbm, ev_hbm, w_hbm, og_hbm, *refs):
    chains = 5 if direct else 4
    out_ev, sums, refs = refs[0], refs[1 : 1 + chains], refs[1 + chains :]
    (
        lens_ref, home_ref, dest_ref, ev_ref,
        w_ref, og_ref, og_t, outbox, inbox, inbox2, pick, place, tok, tok_t, dmix_t,
        slope_t, gate_t, v_t, q_t, k_t, k_z, v_z, attn, slopes, att_t, hgrad_t, mixed_t,
        dout_t, acc, cross, lsem, ssem, rsem, ssem2, rsem2, hs, hr, *bufs,
    ) = refs
    me = lax.axis_index("dp")
    rows, width = ev_ref.shape
    cap = rows // n
    per = width // n
    fold = max(1, 16 // per)
    nq = rows // QB
    bits = n.bit_length() - 1
    group = QB // cap
    head = width // HEADS
    pairs = width // PAIR
    two = PAIR // head
    barrier = enter_all(n, me)
    loads = [
        pltpu.make_async_copy(src, dst, lsem.at[i])
        for i, (src, dst) in enumerate(
            (
                (home_hbm, home_ref),
                (ev_hbm, ev_ref),
                (dest_hbm, dest_ref),
                (og_hbm, og_ref),
                (w_hbm, w_ref),
                (lens_hbm, lens_ref),
            )
        )
    ]
    for load in loads:
        load.start()
    loads[0].wait()
    loads[1].wait()
    there = Exchange(n, me, group, outbox, inbox, ssem, rsem)
    back = Exchange(n, me, group, outbox, inbox2, ssem2, rsem2)

    for k in range(nq):
        at = there.chunk(k)
        part = dot_nn(scatter_chunk(home_ref, at * QB, QB), ev_ref[...]).astype(BF16)
        outbox[pl.ds(at * group, group)] = part.reshape(group, cap, width)
        if k == 0:
            pl.semaphore_wait(barrier, n - 1)
        there.start(k)
    inbox[me] = outbox[me]
    for load in loads[2:]:
        load.wait()
    gather_matrix(dest_ref, pick)

    def prepare(c, carry):
        r = pl.ds(pl.multiple_of(c * QB, QB), QB)
        place[r, :] = scatter_chunk(dest_ref, c * QB, QB)
        x = og_ref[r, :]
        og_t[:, r] = jnp.transpose(x)
        dmix_t[:, r] = (dot_nt(w_ref[:, 4 * width :], x) * 0.5).astype(BF16)
        return carry

    lax.fori_loop(0, nq, prepare, 0)

    def turn_w(c, carry):
        r = pl.ds(pl.multiple_of(c * QB, QB), QB)
        hgrad_t[r, :width] = jnp.transpose(w_ref[:, r]) * 0.5
        return carry

    lax.fori_loop(0, 4 * width // QB, turn_w, 0)

    blocks = rows // BLK
    links = [(i, j) for i in range(blocks) for j in range(i)]
    for x, (i, j) in enumerate(links):
        cross[x] = jnp.full((PAIR, QB), same_owner(lens_ref, j, i), jnp.int32).astype(F32).astype(BF16)

    def linked(value, qc, kc):
        i, j = qc * QB // BLK, kc * QB // BLK
        return value if i == j else value * cross[links.index((i, j))]

    for k in range(nq):
        there.finish(k)
        at = there.chunk(k)
        box = inbox[pl.ds(at * group, group)].reshape(QB, width)
        part = dot_nn(pick[:, pl.ds(pl.multiple_of(at * QB, QB), QB)], box).astype(BF16)
        if k == 0:
            tok[...] = part
        else:
            tok[...] += part

    lane = lax.broadcasted_iota(jnp.int32, (1, PAIR), 1) // head
    picks = [jnp.where(lane == h, 1.0, 0.0).astype(BF16) for h in range(two)]

    def project(c, carry):
        r = pl.ds(pl.multiple_of(c * QB, QB), QB)
        x = tok[r, :]
        for g in range(4):
            rs = slice(g * width, (g + 1) * width)
            u = dot_nt(hgrad_t[rs, :width], x)
            w = jnp.tanh(u) + 1.0
            a = u * w
            low = a.astype(BF16)
            wb = w.astype(BF16)
            slope_t[rs, r] = wb + low * (2.0 - wb)
            if g == 0:
                gate_t[:, r] = low
            elif g == 2:
                q_t[:, :, r] = (low * (0.5 * head**-0.5)).reshape(pairs, PAIR, QB)
            else:
                here, flat = (v_t, v_z) if g == 1 else (k_t, k_z)
                here[:, :, r] = low.reshape(HEADS, head, QB)
                for p in range(pairs):
                    tall = jnp.transpose(low[p * PAIR : (p + 1) * PAIR])
                    for h in range(two):
                        flat[p * two + h, r, :] = tall * picks[h]
        return carry

    lax.fori_loop(0, nq, project, 0)

    tiles = [(qc, kc) for qc in range(nq) for kc in range(qc + 1)]
    low_i = lax.broadcasted_iota(jnp.int32, (QB, QB), 0)
    high_i = lax.broadcasted_iota(jnp.int32, (QB, QB), 1)

    def span(c):
        return slice(c * QB, (c + 1) * QB)

    def forward(p, carry):
        tri = jnp.where(low_i <= high_i, 1.0, 0.0).astype(BF16)
        work = [(h, qc, kc) for h in range(two) for qc, kc in tiles]
        held = {}
        out = None
        for i in range(len(work) + LAG):
            if i < len(work):
                h, qc, kc = work[i]
                q = linked(q_t[p, :, span(qc)], qc, kc)
                held[i] = dot_nn(k_z[p * two + h, span(kc), :], q)
            if i < LAG:
                continue
            h, qc, kc = work[i - LAG]
            u = held.pop(i - LAG)
            g = p * two + h
            w = jnp.tanh(u) + 1.0
            a = (u * w).astype(BF16)
            wb = w.astype(BF16)
            if qc == kc:
                a = a * tri
                wb = wb * tri
            attn[g, tiles.index((qc, kc))] = a
            slopes[g, tiles.index((qc, kc))] = wb
            o = dot_nn(v_t[g, :, span(kc)], a)
            out = o if kc == 0 else out + o
            if qc == kc:
                att_t[g, :, span(qc)] = out
        return carry

    lax.fori_loop(0, pairs, forward, 0)

    def norm(c, carry):
        r = pl.ds(pl.multiple_of(c * 128, 128), 128)
        x = att_t[:, :, r].reshape(width, 128)
        centred = x - jnp.mean(x, axis=0, keepdims=True)
        spread = jnp.mean(centred * centred, axis=0, keepdims=True)
        inv = lax.rsqrt(spread + NORM_EPS)
        unit = centred * inv
        g = gate_t[:, r].astype(F32)
        mixed_t[:, r] = (unit * g).astype(BF16)
        dm = dmix_t[:, r].astype(F32)
        hgrad_t[:width, r] = (dm * unit * slope_t[:width, r].astype(F32)).astype(BF16)
        dn = dm * g
        mean_a = jnp.mean(dn, axis=0, keepdims=True)
        mean_b = jnp.mean(dn * unit, axis=0, keepdims=True)
        dout_t[:, :, r] = (
            (inv * (dn - mean_a - unit * mean_b)).astype(BF16).reshape(pairs, PAIR, 128)
        )
        return carry

    lax.fori_loop(0, rows // 128, norm, 0)

    sources = bufs[:chains]
    hops = bufs[chains:]
    orders = [chain_bits(bits, chain in (1, 2)) for chain in range(chains)]

    def hop(chain, stage):
        bit = orders[chain][stage]
        mine = (me // (1 << bit)) % 2
        peer = me + (1 - 2 * mine) * (1 << bit)
        cur = sources[chain] if stage == 0 else hops[chain * bits + stage - 1]
        got = hops[chain * bits + stage]
        half = cur.shape[0] // 2
        copy = pltpu.make_async_remote_copy(
            src_ref=cur.at[pl.ds((1 - mine) * half, half)],
            dst_ref=got,
            send_sem=hs.at[chain * bits + stage],
            recv_sem=hr.at[chain * bits + stage],
            device_id=(peer,),
            device_id_type=MESH,
        )
        return copy, cur.at[pl.ds(mine * half, half)], got

    columns = chain_columns(width, direct)

    def advance(chain, stage):
        copy, kept, got = hop(chain, stage)
        copy.wait()
        total = kept[...].astype(F32) + got[...].astype(F32)
        if stage == bits - 1:
            sums[chain][...] = total
        else:
            got[...] = total.astype(BF16)
            hop(chain, stage + 1)[0].start()

    def weight_grad(chain):
        order = orders[chain]
        if direct:
            pieces = [
                (start + j, PAIR) for start, size in columns[chain] for j in range(0, size, PAIR)
            ]
            for x in range(0, len(pieces), 2):
                some = pieces[x : x + 2]
                if chain == 1:
                    right = [og_ref[:, lo : lo + size] for lo, size in some]
                    part = dot_nn(mixed_t[...], jnp.concatenate(right, axis=1))
                else:
                    right = [hgrad_t[lo : lo + size, :] for lo, size in some]
                    part = dot_nt(tok_t[...], jnp.concatenate(right, axis=0))
                part = part.astype(BF16)
                cols = slice(x * PAIR, x * PAIR + part.shape[1])
                for slot in range(n):
                    d = slot_device(slot, n, order)
                    sources[chain][slot * per : (slot + 1) * per, cols] = part[d * per : (d + 1) * per]
        else:
            base, size = columns[chain][0]
            thin = size // fold
            step = QB if thin % QB == 0 else thin
            strip = 128

            def fold_rows(x, carry):
                lo = pl.multiple_of(x * strip, strip)
                spot = pl.ds(lo, strip)
                for turn in range(fold):
                    mat = order_block(strip, lo, width, n, per, order, fold, turn)
                    if chain == 1:
                        left = dot_nn(mat, mixed_t[...]).astype(BF16)
                    else:
                        left = dot_nt(mat, tok[...]).astype(BF16)
                    for j in range(thin // step):
                        start = base + turn * thin + j * step
                        if chain == 1:
                            part = dot_nn(left, og_ref[:, start : start + step])
                        else:
                            part = dot_nt(left, hgrad_t[start : start + step, :])
                        cols = slice(j * step, (j + 1) * step)
                        if turn == 0:
                            sources[chain][spot, cols] = part.astype(BF16)
                        else:
                            sources[chain][spot, cols] += part.astype(BF16)
                return carry

            lax.fori_loop(0, n * per * fold // strip, fold_rows, 0)
        hop(chain, 0)[0].start()

    if direct:
        for c in range(nq):
            tok_t[:, span(c)] = jnp.transpose(tok[span(c), :])
    weight_grad(0)
    weight_grad(1)

    def backward(p, carry):
        work = [(h, qc, kc) for h in range(two) for kc in range(nq) for qc in range(kc, nq)]
        held = {}
        ready = {}
        dk = dv = None
        for i in range(len(work) + BACK_LAG + DEEP):
            if i < len(work):
                h, qc, kc = work[i]
                d = linked(dout_t[p, :, span(qc)], qc, kc)
                held[i] = dot_nn(v_z[p * two + h, span(kc), :], d)
            j = i - BACK_LAG
            if 0 <= j < len(work):
                h, qc, kc = work[j]
                a = attn[p * two + h, tiles.index((qc, kc))]
                wb = slopes[p * two + h, tiles.index((qc, kc))]
                ready[j] = held.pop(j).astype(BF16) * (wb + a * (2.0 - wb))
            j = i - BACK_LAG - DEEP
            if j < 0:
                continue
            h, qc, kc = work[j]
            ds = ready.pop(j)
            g = p * two + h
            mine = slice(h * head, (h + 1) * head)
            dq = dot_nn(k_t[g, :, span(kc)], ds)
            if kc == 0:
                acc[h, :, span(qc)] = dq
            else:
                acc[h, :, span(qc)] += dq
            more_k = dot_nt(q_t[p, mine, span(qc)], ds)
            more_v = dot_nt(dout_t[p, mine, span(qc)], attn[g, tiles.index((qc, kc))])
            dk = more_k if qc == kc else dk + more_k
            dv = more_v if qc == kc else dv + more_v
            if qc == nq - 1:
                for grp, val in ((1, dv), (3, dk)):
                    rs = pl.ds(pl.multiple_of(grp * width + p * PAIR + h * head, head), head)
                    hgrad_t[rs, span(kc)] = (
                        val.astype(BF16).astype(F32) * slope_t[rs, span(kc)].astype(F32)
                    ).astype(BF16)
            if kc == qc:
                rs = pl.ds(pl.multiple_of(2 * width + p * PAIR + h * head, head), head)
                full = (acc[h, :, span(qc)] * (0.5 * head**-0.5)).astype(BF16).astype(F32)
                hgrad_t[rs, span(qc)] = (full * slope_t[rs, span(qc)].astype(F32)).astype(BF16)

        @pl.when(p == 0)
        def _():
            advance(0, 0)
            advance(1, 0)

        if direct:

            @pl.when(p == pairs - 3)
            def _():
                weight_grad(2)
                advance(0, 1)
                advance(1, 1)

        @pl.when(p == pairs - 2)
        def _():
            if direct:
                advance(2, 0)
                weight_grad(3)
                advance(0, 2)
                advance(1, 2)

        @pl.when(p == pairs - 1)
        def _():
            if direct:
                advance(3, 0)
                advance(0, 3)
                advance(1, 3)
            else:
                for stage in (1, 2):
                    advance(0, stage)
                    advance(1, stage)

        return carry

    lax.fori_loop(0, pairs, backward, 0)

    def tokens_back(c, carry):
        r = pl.ds(pl.multiple_of(c * QB, QB), QB)
        dmix_t[:, r] = (
            og_t[:, r].astype(F32) + dot_nn(w_ref[:, : 4 * width], hgrad_t[:, r])
        ).astype(BF16)
        return carry

    lax.fori_loop(0, nq, tokens_back, 0)

    if direct:
        pass
    def fill_back(k):
        at = back.chunk(k)
        r = pl.ds(pl.multiple_of(at * QB, QB), QB)
        part = dot_nt(place[r, :], dmix_t[...]).astype(BF16)
        outbox[pl.ds(at * group, group)] = part.reshape(group, cap, width)

    stores = []

    def collect(k, first=False, last=False):
        back.arrived(k)
        at = back.chunk(k)
        box = inbox2[pl.ds(at * group, group)].reshape(QB, width)
        cols = pl.ds(pl.multiple_of(at * QB, QB), QB)
        if not last:
            part = dot_nn(pick[:, cols], box).astype(BF16)
            tok[...] = part if first else tok[...] + part
            return
        for c in range(nq):
            tok[span(c), :] += dot_nn(pick[span(c), cols], box).astype(BF16)
            stores.append(
                pltpu.make_async_copy(tok.at[span(c)], out_ev.at[span(c)], lsem.at[c])
            )
            stores[-1].start()

    plan = PLAN if direct else WHOLE_PLAN
    for what, *args in plan:
        if what == "fill":
            fill_back(*args)
        elif what == "start":
            back.start(*args)
        elif what == "sent":
            back.sent(*args)
        elif what == "msg":
            back.copy(*args).start()
        elif what == "gone":
            back.copy(*args).wait_send()
        elif what == "get":
            collect(*args)
        elif what == "own":
            inbox2[me] = outbox[me]
        elif what == "grad":
            weight_grad(*args)
        elif what == "pick":
            gather_matrix(home_ref, pick)
        else:
            advance(*args)
    inbox2[me] = outbox[me]
    for store in stores:
        store.wait()


def chain_columns(width, direct):
    half = width // 2
    if not direct:
        return [[(0, width)], [(0, width)], [(width, 3 * half)], [(width + 3 * half, 3 * half)]]
    parts = ((0, half), (half, PAIR), (half + PAIR, PAIR))
    late = [[(width * g + at, size) for g in (1, 2, 3)] for at, size in parts]
    return [[(0, width)], [(0, width)], *late]


def finish_kernel(scale, columns, count, *refs):
    wide, spots, scratch = refs[: count + 3], refs[count + 3 : count + 6], refs[count + 6 :]
    ev_hbm, *small = wide
    held, *near, ni_ref, no_ref, isem, osem, psem = scratch
    loads, stores = [], []
    parts = osem.shape[0] - 2
    size = held.shape[0] // parts
    for i in range(parts):
        r = pl.ds(i * size, size)
        loads.append(pltpu.make_async_copy(ev_hbm.at[r], held.at[r], isem.at[i]))
        stores.append(pltpu.make_async_copy(held.at[r], spots[0].at[r], osem.at[i]))
    other = [
        pltpu.make_async_copy(src, dst, psem.at[i]) for i, (src, dst) in enumerate(zip(small, near))
    ]
    for load in [*other, *loads]:
        load.start()
    for load in other:
        load.wait()
    *sums, mi_ref, mo_ref = near
    no_ref[...] = DECAY * mo_ref[...] + scale * sums[1][...]
    for chain in range(count):
        if chain == 1:
            continue
        at = 0
        for start, span in columns[chain]:
            cols = slice(start, start + span)
            ni_ref[:, cols] = DECAY * mi_ref[:, cols] + scale * sums[chain][:, at : at + span]
            at += span
    stores.append(pltpu.make_async_copy(ni_ref, spots[1], osem.at[parts]))
    stores.append(pltpu.make_async_copy(no_ref, spots[2], osem.at[parts + 1]))
    stores[-1].start()
    stores[-2].start()
    for load, store in zip(loads, stores):
        load.wait()
        store.start()
    for store in stores:
        store.wait()


def shards(n, events, home_slot, dest_slot, seq_lens, weights, out_grad, momentum_in, momentum_out):
    rows, width = events.shape
    cap = rows // n
    bits = n.bit_length() - 1
    per = width // n
    fold = max(1, 16 // per)
    tall = per * fold
    direct = fold == 1
    nq = rows // QB
    pairs = width // PAIR
    head = width // HEADS
    scale = (n * rows) ** (-0.5)
    home = home_slot.reshape(1, rows)
    dest = dest_slot.reshape(1, rows)
    vm = pl.BlockSpec(memory_space=pltpu.VMEM)
    sm = pl.BlockSpec(memory_space=pltpu.SMEM)
    hbm = pl.BlockSpec(memory_space=pl.ANY)
    dma = pltpu.SemaphoreType.DMA
    columns = chain_columns(width, direct)
    wides = [sum(size for _, size in cols) for cols in columns]
    thins = [w // fold for w in wides]
    bufs = [pltpu.VMEM((n * tall, t), BF16) for t in thins]
    for t in thins:
        for stage in range(bits):
            bufs.append(pltpu.VMEM((n * tall >> (stage + 1), t), BF16))

    def area(*shape, kind=BF16):
        return pltpu.VMEM(shape, kind)

    boxed = area(n, cap, width)
    ntile = nq * (nq + 1) // 2
    blocks = rows // BLK
    ev_shape = jax.ShapeDtypeStruct(events.shape, BF16)
    ev, *parts = pl.pallas_call(
        functools.partial(step_kernel, n, direct),
        out_shape=[ev_shape] + [jax.ShapeDtypeStruct((tall, t), F32) for t in thins],
        in_specs=[hbm] * 6,
        out_specs=[hbm] + [vm] * len(thins),
        scratch_shapes=[
            pltpu.SMEM(seq_lens.shape, jnp.int32),
            area(1, rows, kind=jnp.int32),
            area(1, rows, kind=jnp.int32),
            area(rows, width),
            area(width, 5 * width),
            area(rows, width),
            area(width, rows),
            boxed,
            boxed,
            boxed,
            area(rows, rows),
            area(rows, rows),
            area(rows, width),
            area(width, rows),
            area(width, rows),
            area(4 * width, rows),
            area(width, rows),
            area(HEADS, head, rows),
            area(pairs, PAIR, rows),
            area(HEADS, head, rows),
            area(HEADS, rows, PAIR),
            area(HEADS, rows, PAIR),
            area(HEADS, ntile, QB, QB),
            area(HEADS, ntile, QB, QB),
            area(HEADS, head, rows, kind=F32),
            area(4 * width, rows),
            area(width, rows),
            area(pairs, PAIR, rows),
            area(PAIR // head, head, rows, kind=F32),
            area(max(1, blocks * (blocks - 1) // 2), PAIR, QB),
            dma((6,)),
            dma((n,)),
            dma((n,)),
            dma((n,)),
            dma((n,)),
            dma((len(thins) * bits,)),
            dma((len(thins) * bits,)),
        ]
        + bufs,
        compiler_params=pltpu.CompilerParams(
            collective_id=0, has_side_effects=True, vmem_limit_bytes=VMEM_LIMIT
        ),
        name="step",
    )(seq_lens, home, dest, events, weights, out_grad)
    if not direct:
        parts = [
            f.reshape(fold, per, f.shape[1]).transpose(1, 0, 2).reshape(per, fold * f.shape[1])
            for f in parts
        ]
    small = (*parts, momentum_in, momentum_out)
    return pl.pallas_call(
        functools.partial(finish_kernel, scale, columns, len(parts)),
        out_shape=[
            ev_shape,
            jax.ShapeDtypeStruct(momentum_in.shape, F32),
            jax.ShapeDtypeStruct(momentum_out.shape, F32),
        ],
        in_specs=[hbm] * (len(small) + 1),
        out_specs=[hbm] * 3,
        scratch_shapes=[
            area(rows, width),
            *(area(*x.shape, kind=F32) for x in small),
            area(*momentum_in.shape, kind=F32),
            area(*momentum_out.shape, kind=F32),
            dma((4,)),
            dma((6,)),
            dma((len(small),)),
        ],
        compiler_params=pltpu.CompilerParams(vmem_limit_bytes=VMEM_LIMIT),
        name="finish",
    )(ev, *small)


def solution(mesh):
    n = mesh.shape["dp"]
    row = P("dp", None)
    return jax.shard_map(
        functools.partial(shards, n),
        mesh=mesh,
        in_specs=(row, P("dp"), P("dp"), P("dp"), P(), row, row, row),
        out_specs=(row, row, row),
        check_vma=False,
    )
```

```python
import functools

import jax
import jax.numpy as jnp
from jax import lax
from jax.experimental import pallas as pl
from jax.experimental.pallas import tpu as pltpu
from jax.sharding import PartitionSpec as P

HEADS = 8
BLK = 512
QB = 256
PAIR = 128
NORM_EPS = 1e-05
DECAY = 0.9
MESH = pl.DeviceIdType.MESH
F32 = jnp.float32
BF16 = jnp.bfloat16
VMEM_LIMIT = 67 * 1000 * 1000
LAG = 4
BACK_LAG = 2
DEEP = 1
LATE = ((4, 0), (3, 1), (2, 2), (4, 1), (0, 4), (1, 4), (3, 2), (2, 3), (4, 2), (3, 3), (2, 4), (4, 3), (3, 4), (4, 4))
PLAN = (('fill', 3), ('fill', 1), ('msg', 3, 0), ('msg', 1, 0), ('msg', 3, 1), ('msg', 1, 1), ('msg', 3, 2), ('msg', 1, 2), ('msg', 3, 3), ('msg', 1, 3), ('fill', 0), ('fill', 2), ('own',), ('msg', 3, 4), ('msg', 1, 4), ('msg', 3, 5), ('msg', 1, 5), ('grad', 4), ('gone', 3, 0), ('gone', 1, 0), ('msg', 3, 6), ('msg', 1, 6), ('add', 2, 1), ('add', 3, 1), ('gone', 3, 1), ('gone', 1, 1), ('msg', 3, 7), ('msg', 1, 7), ('add', 4, 0), ('gone', 3, 2), ('gone', 1, 2), ('msg', 2, 0), ('msg', 0, 1), ('add', 0, 4), ('add', 1, 4), ('gone', 3, 3), ('gone', 1, 3), ('msg', 2, 1), ('msg', 0, 2), ('pick',), ('add', 2, 2), ('add', 4, 1), ('add', 3, 2), ('gone', 3, 4), ('gone', 1, 4), ('msg', 2, 2), ('msg', 0, 3), ('add', 2, 3), ('gone', 3, 5), ('gone', 1, 5), ('msg', 2, 3), ('msg', 0, 4), ('add', 4, 2), ('add', 3, 3), ('gone', 3, 6), ('gone', 1, 6), ('msg', 2, 4), ('msg', 0, 5), ('gone', 3, 7), ('gone', 1, 7), ('msg', 2, 5), ('msg', 0, 6), ('get', 1, True), ('add', 2, 4), ('add', 4, 3), ('add', 3, 4), ('gone', 2, 0), ('gone', 0, 1), ('msg', 2, 6), ('msg', 0, 7), ('gone', 2, 1), ('gone', 0, 2), ('msg', 2, 7), ('get', 0), ('get', 3), ('add', 4, 4), ('get', 2, False, True), ('gone', 2, 2), ('gone', 0, 3), ('gone', 2, 3), ('gone', 0, 4), ('gone', 2, 4), ('gone', 0, 5), ('gone', 2, 5), ('gone', 0, 6), ('gone', 2, 6), ('gone', 0, 7), ('gone', 2, 7))
WHOLE_PLAN = (
    *((what, k) for k in range(4) for what in ("fill", "start")),
    ("grad", 2),
    ("grad", 3),
    ("pick",),
    *(("add", chain, stage) for stage in (3, 4, 5, 6) for chain in (0, 1)),
    *(("add", chain, stage) for stage in range(7) for chain in (2, 3)),
    ("own",),
    ("get", 0, True),
    ("get", 1),
    ("get", 2),
    ("get", 3, False, True),
    *(("sent", k) for k in range(4)),
)


def dot_nn(a, b):
    return lax.dot_general(a, b, (((1,), (0,)), ((), ())), preferred_element_type=F32)


def dot_nt(a, b):
    return lax.dot_general(a, b, (((1,), (1,)), ((), ())), preferred_element_type=F32)


def chain_bits(bit_count, second):
    order = list(range(bit_count))
    if second and bit_count > 2:
        order[1], order[2] = order[2], order[1]
    return order


def slot_device(slot, n, bits):
    return sum(((slot // (n >> (rank + 1))) % 2) << bit for rank, bit in enumerate(bits))


def enter_all(n, me):
    barrier = pltpu.get_barrier_semaphore()

    def greet(i, carry):
        pl.semaphore_signal(barrier, inc=1, device_id=((me + i) % n,), device_id_type=MESH)
        return carry

    lax.fori_loop(1, n, greet, 0)
    return barrier


def flip(value, other, size):
    total = 0
    weight = 1
    while weight < size:
        total = total + (value // weight + other // weight) % 2 * weight
        weight *= 2
    return total


class Exchange:
    def __init__(self, n, me, group, src, dst, ssem, rsem):
        self.n, self.me, self.group = n, me, group
        self.src, self.dst, self.ssem, self.rsem = src, dst, ssem, rsem

    def chunk(self, k):
        return flip(self.me // self.group, k, self.n // self.group)

    def copy(self, k, j):
        peer = self.chunk(k) * self.group + flip(self.me % self.group, j, self.group)
        i = k * self.group + j
        return pltpu.make_async_remote_copy(
            src_ref=self.src.at[peer],
            dst_ref=self.dst.at[self.me],
            send_sem=self.ssem.at[i],
            recv_sem=self.rsem.at[i],
            device_id=(peer,),
            device_id_type=MESH,
        )

    def each(self, k, act):
        def go(j, carry):
            act(self.copy(k, j))
            return carry

        lax.fori_loop(1 if k == 0 else 0, self.group, go, 0)

    def start(self, k):
        self.each(k, lambda copy: copy.start())

    def sent(self, k):
        self.each(k, lambda copy: copy.wait_send())

    def arrived(self, k):
        self.each(k, lambda copy: copy.wait_recv())

    def finish(self, k):
        self.each(k, lambda copy: copy.wait())


def gather_matrix(slots_ref, out_ref):
    rows = out_ref.shape[0]
    wide = jnp.broadcast_to(slots_ref[...].astype(F32), (128, rows))
    column = jnp.transpose(wide)
    lane = lax.broadcasted_iota(jnp.int32, (rows, 128), 1).astype(F32)
    for j in range(rows // 128):
        out_ref[:, j * 128 : (j + 1) * 128] = jnp.where(
            column == lane + float(j * 128), 1.0, 0.0
        ).astype(BF16)


def scatter_chunk(slots_ref, start, size):
    rows = slots_ref.shape[1]
    place = lax.broadcasted_iota(jnp.int32, (size, rows), 0) + start
    return jnp.where(place == slots_ref[...], 1.0, 0.0).astype(BF16)


def same_owner(lens_ref, low, high):
    start = 0
    same = 0
    for j in range(lens_ref.shape[0]):
        blocks = (lens_ref[j] + BLK - 1) // BLK
        inside = jnp.where((start <= low) & (high < start + blocks), 1, 0)
        same = same + inside
        start = start + blocks
    return same


def order_block(height, base, width, n, per, bits, fold, turn):
    shape = (height, width)
    tall = per * fold
    place = lax.broadcasted_iota(jnp.int32, shape, 0) + base
    column = lax.broadcasted_iota(jnp.int32, shape, 1)
    slot = place // tall
    rest = place % tall
    device = jnp.zeros(shape, jnp.int32)
    for rank, bit in enumerate(bits):
        weight = n >> (rank + 1)
        device = device + ((slot // weight) % 2) * (1 << bit)
    hit = (column == device * per + rest % per) & (rest // per == turn)
    return jnp.where(hit, 1.0, 0.0).astype(BF16)


def step_kernel(n, direct, lens_hbm, home_hbm, dest_hbm, ev_hbm, w_hbm, og_hbm, *refs):
    chains = 5 if direct else 4
    out_ev, sums, refs = refs[0], refs[1 : 1 + chains], refs[1 + chains :]
    (
        lens_ref, home_ref, dest_ref, ev_ref,
        w_ref, og_ref, og_t, outbox, inbox, inbox2, pick, place, tok, tok_t, dmix_t,
        slope_t, gate_t, v_t, q_t, k_t, k_z, v_z, attn, slopes, att_t, hgrad_t, mixed_t,
        dout_t, acc, cross, lsem, ssem, rsem, ssem2, rsem2, hs, hr, *bufs,
    ) = refs
    me = lax.axis_index("dp")
    rows, width = ev_ref.shape
    cap = rows // n
    per = width // n
    fold = max(1, 16 // per)
    nq = rows // QB
    bits = n.bit_length() - 1
    group = QB // cap
    head = width // HEADS
    pairs = width // PAIR
    two = PAIR // head
    barrier = enter_all(n, me)
    loads = [
        pltpu.make_async_copy(src, dst, lsem.at[i])
        for i, (src, dst) in enumerate(
            (
                (home_hbm, home_ref),
                (ev_hbm, ev_ref),
                (dest_hbm, dest_ref),
                (og_hbm, og_ref),
                (w_hbm, w_ref),
                (lens_hbm, lens_ref),
            )
        )
    ]
    for load in loads:
        load.start()
    loads[0].wait()
    loads[1].wait()
    there = Exchange(n, me, group, outbox, inbox, ssem, rsem)
    back = Exchange(n, me, group, outbox, inbox2, ssem2, rsem2)

    for k in range(nq):
        at = there.chunk(k)
        part = dot_nn(scatter_chunk(home_ref, at * QB, QB), ev_ref[...]).astype(BF16)
        outbox[pl.ds(at * group, group)] = part.reshape(group, cap, width)
    pl.semaphore_wait(barrier, n - 1)
    for k in (*range(nq // 2, nq), *range(nq // 2 - 1, -1, -1)):
        there.start(k)
    inbox[me] = outbox[me]
    for load in loads[2:]:
        load.wait()
    gather_matrix(dest_ref, pick)

    def prepare(c, carry):
        r = pl.ds(pl.multiple_of(c * QB, QB), QB)
        place[r, :] = scatter_chunk(dest_ref, c * QB, QB)
        x = og_ref[r, :]
        og_t[:, r] = jnp.transpose(x)
        dmix_t[:, r] = (dot_nt(w_ref[:, 4 * width :], x) * 0.5).astype(BF16)
        return carry

    lax.fori_loop(0, nq, prepare, 0)

    def turn_w(c, carry):
        r = pl.ds(pl.multiple_of(c * QB, QB), QB)
        hgrad_t[r, :width] = jnp.transpose(w_ref[:, r]) * 0.5
        return carry

    lax.fori_loop(0, 4 * width // QB, turn_w, 0)

    blocks = rows // BLK
    links = [(i, j) for i in range(blocks) for j in range(i)]
    for x, (i, j) in enumerate(links):
        cross[x] = jnp.full((PAIR, QB), same_owner(lens_ref, j, i), jnp.int32).astype(F32).astype(BF16)

    def linked(value, qc, kc):
        i, j = qc * QB // BLK, kc * QB // BLK
        return value if i == j else value * cross[links.index((i, j))]

    for k in range(nq):
        there.finish(k)
        at = there.chunk(k)
        box = inbox[pl.ds(at * group, group)].reshape(QB, width)
        part = dot_nn(pick[:, pl.ds(pl.multiple_of(at * QB, QB), QB)], box).astype(BF16)
        if k == 0:
            tok[...] = part
        else:
            tok[...] += part

    lane = lax.broadcasted_iota(jnp.int32, (1, PAIR), 1) // head
    picks = [jnp.where(lane == h, 1.0, 0.0).astype(BF16) for h in range(two)]

    def project(c, carry):
        r = pl.ds(pl.multiple_of(c * QB, QB), QB)
        x = tok[r, :]
        for g in range(4):
            rs = slice(g * width, (g + 1) * width)
            u = dot_nt(hgrad_t[rs, :width], x)
            w = jnp.tanh(u) + 1.0
            a = u * w
            low = a.astype(BF16)
            wb = w.astype(BF16)
            slope_t[rs, r] = wb + low * (2.0 - wb)
            if g == 0:
                gate_t[:, r] = low
            elif g == 2:
                q_t[:, :, r] = (low * (0.5 * head**-0.5)).reshape(pairs, PAIR, QB)
            else:
                here, flat = (v_t, v_z) if g == 1 else (k_t, k_z)
                here[:, :, r] = low.reshape(HEADS, head, QB)
                for p in range(pairs):
                    tall = jnp.transpose(low[p * PAIR : (p + 1) * PAIR])
                    for h in range(two):
                        flat[p * two + h, r, :] = tall * picks[h]
        return carry

    lax.fori_loop(0, nq, project, 0)

    tiles = [(qc, kc) for qc in range(nq) for kc in range(qc + 1)]
    low_i = lax.broadcasted_iota(jnp.int32, (QB, QB), 0)
    high_i = lax.broadcasted_iota(jnp.int32, (QB, QB), 1)

    def span(c):
        return slice(c * QB, (c + 1) * QB)

    def forward(p, carry):
        tri = jnp.where(low_i <= high_i, 1.0, 0.0).astype(BF16)
        work = [(h, qc, kc) for h in range(two) for qc, kc in tiles]
        held = {}
        out = None
        for i in range(len(work) + LAG):
            if i < len(work):
                h, qc, kc = work[i]
                q = linked(q_t[p, :, span(qc)], qc, kc)
                held[i] = dot_nn(k_z[p * two + h, span(kc), :], q)
            if i < LAG:
                continue
            h, qc, kc = work[i - LAG]
            u = held.pop(i - LAG)
            g = p * two + h
            w = jnp.tanh(u) + 1.0
            a = (u * w).astype(BF16)
            wb = w.astype(BF16)
            if qc == kc:
                a = a * tri
                wb = wb * tri
            attn[g, tiles.index((qc, kc))] = a
            slopes[g, tiles.index((qc, kc))] = wb
            o = dot_nn(v_t[g, :, span(kc)], a)
            out = o if kc == 0 else out + o
            if qc == kc:
                att_t[g, :, span(qc)] = out
        return carry

    lax.fori_loop(0, pairs, forward, 0)

    def norm(c, carry):
        r = pl.ds(pl.multiple_of(c * 128, 128), 128)
        x = att_t[:, :, r].reshape(width, 128)
        centred = x - jnp.mean(x, axis=0, keepdims=True)
        spread = jnp.mean(centred * centred, axis=0, keepdims=True)
        inv = lax.rsqrt(spread + NORM_EPS)
        unit = centred * inv
        g = gate_t[:, r].astype(F32)
        mixed_t[:, r] = (unit * g).astype(BF16)
        dm = dmix_t[:, r].astype(F32)
        hgrad_t[:width, r] = (dm * unit * slope_t[:width, r].astype(F32)).astype(BF16)
        dn = dm * g
        mean_a = jnp.mean(dn, axis=0, keepdims=True)
        mean_b = jnp.mean(dn * unit, axis=0, keepdims=True)
        dout_t[:, :, r] = (
            (inv * (dn - mean_a - unit * mean_b)).astype(BF16).reshape(pairs, PAIR, 128)
        )
        return carry

    lax.fori_loop(0, rows // 128, norm, 0)

    sources = bufs[:chains]
    hops = bufs[chains:]
    orders = [chain_bits(bits, chain in (1, 2)) for chain in range(chains)]

    def hop(chain, stage):
        bit = orders[chain][stage]
        mine = (me // (1 << bit)) % 2
        peer = me + (1 - 2 * mine) * (1 << bit)
        cur = sources[chain] if stage == 0 else hops[chain * bits + stage - 1]
        got = hops[chain * bits + stage]
        half = cur.shape[0] // 2
        copy = pltpu.make_async_remote_copy(
            src_ref=cur.at[pl.ds((1 - mine) * half, half)],
            dst_ref=got,
            send_sem=hs.at[chain * bits + stage],
            recv_sem=hr.at[chain * bits + stage],
            device_id=(peer,),
            device_id_type=MESH,
        )
        return copy, cur.at[pl.ds(mine * half, half)], got

    columns = chain_columns(width, direct)

    def advance(chain, stage):
        copy, kept, got = hop(chain, stage)
        copy.wait()
        total = kept[...].astype(F32) + got[...].astype(F32)
        if stage == bits - 1:
            sums[chain][...] = total
        else:
            got[...] = total.astype(BF16)
            hop(chain, stage + 1)[0].start()

    def weight_grad(chain):
        order = orders[chain]
        if direct:
            pieces = [
                (start + j, PAIR) for start, size in columns[chain] for j in range(0, size, PAIR)
            ]
            for x in range(0, len(pieces), 2):
                some = pieces[x : x + 2]
                if chain == 1:
                    right = [og_ref[:, lo : lo + size] for lo, size in some]
                    part = dot_nn(mixed_t[...], jnp.concatenate(right, axis=1))
                else:
                    right = [hgrad_t[lo : lo + size, :] for lo, size in some]
                    part = dot_nt(tok_t[...], jnp.concatenate(right, axis=0))
                part = part.astype(BF16)
                cols = slice(x * PAIR, x * PAIR + part.shape[1])
                for slot in range(n):
                    d = slot_device(slot, n, order)
                    sources[chain][slot * per : (slot + 1) * per, cols] = part[d * per : (d + 1) * per]
        else:
            base, size = columns[chain][0]
            thin = size // fold
            step = QB if thin % QB == 0 else thin
            strip = 128

            def fold_rows(x, carry):
                lo = pl.multiple_of(x * strip, strip)
                spot = pl.ds(lo, strip)
                for turn in range(fold):
                    mat = order_block(strip, lo, width, n, per, order, fold, turn)
                    if chain == 1:
                        left = dot_nn(mat, mixed_t[...]).astype(BF16)
                    else:
                        left = dot_nt(mat, tok[...]).astype(BF16)
                    for j in range(thin // step):
                        start = base + turn * thin + j * step
                        if chain == 1:
                            part = dot_nn(left, og_ref[:, start : start + step])
                        else:
                            part = dot_nt(left, hgrad_t[start : start + step, :])
                        cols = slice(j * step, (j + 1) * step)
                        if turn == 0:
                            sources[chain][spot, cols] = part.astype(BF16)
                        else:
                            sources[chain][spot, cols] += part.astype(BF16)
                return carry

            lax.fori_loop(0, n * per * fold // strip, fold_rows, 0)
        hop(chain, 0)[0].start()

    if direct:
        for c in range(nq):
            tok_t[:, span(c)] = jnp.transpose(tok[span(c), :])
    weight_grad(0)
    weight_grad(1)

    def backward(p, carry):
        work = [(h, qc, kc) for h in range(two) for kc in range(nq) for qc in range(kc, nq)]
        held = {}
        ready = {}
        dk = dv = None
        for i in range(len(work) + BACK_LAG + DEEP):
            if i < len(work):
                h, qc, kc = work[i]
                d = linked(dout_t[p, :, span(qc)], qc, kc)
                held[i] = dot_nn(v_z[p * two + h, span(kc), :], d)
            j = i - BACK_LAG
            if 0 <= j < len(work):
                h, qc, kc = work[j]
                a = attn[p * two + h, tiles.index((qc, kc))]
                wb = slopes[p * two + h, tiles.index((qc, kc))]
                ready[j] = held.pop(j).astype(BF16) * (wb + a * (2.0 - wb))
            j = i - BACK_LAG - DEEP
            if j < 0:
                continue
            h, qc, kc = work[j]
            ds = ready.pop(j)
            g = p * two + h
            mine = slice(h * head, (h + 1) * head)
            dq = dot_nn(k_t[g, :, span(kc)], ds)
            if kc == 0:
                acc[h, :, span(qc)] = dq
            else:
                acc[h, :, span(qc)] += dq
            more_k = dot_nt(q_t[p, mine, span(qc)], ds)
            more_v = dot_nt(dout_t[p, mine, span(qc)], attn[g, tiles.index((qc, kc))])
            dk = more_k if qc == kc else dk + more_k
            dv = more_v if qc == kc else dv + more_v
            if qc == nq - 1:
                for grp, val in ((1, dv), (3, dk)):
                    rs = pl.ds(pl.multiple_of(grp * width + p * PAIR + h * head, head), head)
                    hgrad_t[rs, span(kc)] = (
                        val.astype(BF16).astype(F32) * slope_t[rs, span(kc)].astype(F32)
                    ).astype(BF16)
            if kc == qc:
                rs = pl.ds(pl.multiple_of(2 * width + p * PAIR + h * head, head), head)
                full = (acc[h, :, span(qc)] * (0.5 * head**-0.5)).astype(BF16).astype(F32)
                hgrad_t[rs, span(qc)] = (full * slope_t[rs, span(qc)].astype(F32)).astype(BF16)

        @pl.when(p == 0)
        def _():
            advance(0, 0)
            advance(1, 0)

        if direct:

            @pl.when(p == pairs - 3)
            def _():
                weight_grad(2)
                advance(0, 1)
                advance(1, 1)

        @pl.when(p == pairs - 2)
        def _():
            if direct:
                advance(2, 0)
                weight_grad(3)
                advance(0, 2)
                advance(1, 2)

        @pl.when(p == pairs - 1)
        def _():
            if direct:
                advance(3, 0)
                advance(0, 3)
                advance(1, 3)
            else:
                for stage in (1, 2):
                    advance(0, stage)
                    advance(1, stage)

        return carry

    lax.fori_loop(0, pairs, backward, 0)

    def tokens_back(c, carry):
        r = pl.ds(pl.multiple_of(c * QB, QB), QB)
        dmix_t[:, r] = (
            og_t[:, r].astype(F32) + dot_nn(w_ref[:, : 4 * width], hgrad_t[:, r])
        ).astype(BF16)
        return carry

    lax.fori_loop(0, nq, tokens_back, 0)

    if direct:
        pass
    def fill_back(k):
        at = back.chunk(k)
        r = pl.ds(pl.multiple_of(at * QB, QB), QB)
        part = dot_nt(place[r, :], dmix_t[...]).astype(BF16)
        outbox[pl.ds(at * group, group)] = part.reshape(group, cap, width)

    stores = []

    def collect(k, first=False, last=False):
        back.arrived(k)
        at = back.chunk(k)
        box = inbox2[pl.ds(at * group, group)].reshape(QB, width)
        cols = pl.ds(pl.multiple_of(at * QB, QB), QB)
        if not last:
            part = dot_nn(pick[:, cols], box).astype(BF16)
            tok[...] = part if first else tok[...] + part
            return
        for c in range(nq):
            tok[span(c), :] += dot_nn(pick[span(c), cols], box).astype(BF16)
            stores.append(
                pltpu.make_async_copy(tok.at[span(c)], out_ev.at[span(c)], lsem.at[c])
            )
            stores[-1].start()

    plan = PLAN if direct else WHOLE_PLAN
    for what, *args in plan:
        if what == "fill":
            fill_back(*args)
        elif what == "start":
            back.start(*args)
        elif what == "sent":
            back.sent(*args)
        elif what == "msg":
            back.copy(*args).start()
        elif what == "gone":
            back.copy(*args).wait_send()
        elif what == "get":
            collect(*args)
        elif what == "own":
            inbox2[me] = outbox[me]
        elif what == "grad":
            weight_grad(*args)
        elif what == "pick":
            gather_matrix(home_ref, pick)
        else:
            advance(*args)
    inbox2[me] = outbox[me]
    for store in stores:
        store.wait()


def chain_columns(width, direct):
    half = width // 2
    if not direct:
        return [[(0, width)], [(0, width)], [(width, 3 * half)], [(width + 3 * half, 3 * half)]]
    parts = ((0, half), (half, PAIR), (half + PAIR, PAIR))
    late = [[(width * g + at, size) for g in (1, 2, 3)] for at, size in parts]
    return [[(0, width)], [(0, width)], *late]


def finish_kernel(scale, columns, count, *refs):
    wide, spots, scratch = refs[: count + 3], refs[count + 3 : count + 6], refs[count + 6 :]
    ev_hbm, *small = wide
    held, *near, ni_ref, no_ref, isem, osem, psem = scratch
    loads, stores = [], []
    parts = osem.shape[0] - 2
    size = held.shape[0] // parts
    for i in range(parts):
        r = pl.ds(i * size, size)
        loads.append(pltpu.make_async_copy(ev_hbm.at[r], held.at[r], isem.at[i]))
        stores.append(pltpu.make_async_copy(held.at[r], spots[0].at[r], osem.at[i]))
    other = [
        pltpu.make_async_copy(src, dst, psem.at[i]) for i, (src, dst) in enumerate(zip(small, near))
    ]
    for load in [*other, *loads]:
        load.start()
    for load in other:
        load.wait()
    *sums, mi_ref, mo_ref = near
    no_ref[...] = DECAY * mo_ref[...] + scale * sums[1][...]
    for chain in range(count):
        if chain == 1:
            continue
        at = 0
        for start, span in columns[chain]:
            cols = slice(start, start + span)
            ni_ref[:, cols] = DECAY * mi_ref[:, cols] + scale * sums[chain][:, at : at + span]
            at += span
    stores.append(pltpu.make_async_copy(ni_ref, spots[1], osem.at[parts]))
    stores.append(pltpu.make_async_copy(no_ref, spots[2], osem.at[parts + 1]))
    stores[-1].start()
    stores[-2].start()
    for load, store in zip(loads, stores):
        load.wait()
        store.start()
    for store in stores:
        store.wait()


def shards(n, events, home_slot, dest_slot, seq_lens, weights, out_grad, momentum_in, momentum_out):
    rows, width = events.shape
    cap = rows // n
    bits = n.bit_length() - 1
    per = width // n
    fold = max(1, 16 // per)
    tall = per * fold
    direct = fold == 1
    nq = rows // QB
    pairs = width // PAIR
    head = width // HEADS
    scale = (n * rows) ** (-0.5)
    home = home_slot.reshape(1, rows)
    dest = dest_slot.reshape(1, rows)
    vm = pl.BlockSpec(memory_space=pltpu.VMEM)
    sm = pl.BlockSpec(memory_space=pltpu.SMEM)
    hbm = pl.BlockSpec(memory_space=pl.ANY)
    dma = pltpu.SemaphoreType.DMA
    columns = chain_columns(width, direct)
    wides = [sum(size for _, size in cols) for cols in columns]
    thins = [w // fold for w in wides]
    bufs = [pltpu.VMEM((n * tall, t), BF16) for t in thins]
    for t in thins:
        for stage in range(bits):
            bufs.append(pltpu.VMEM((n * tall >> (stage + 1), t), BF16))

    def area(*shape, kind=BF16):
        return pltpu.VMEM(shape, kind)

    boxed = area(n, cap, width)
    ntile = nq * (nq + 1) // 2
    blocks = rows // BLK
    ev_shape = jax.ShapeDtypeStruct(events.shape, BF16)
    ev, *parts = pl.pallas_call(
        functools.partial(step_kernel, n, direct),
        out_shape=[ev_shape] + [jax.ShapeDtypeStruct((tall, t), F32) for t in thins],
        in_specs=[hbm] * 6,
        out_specs=[hbm] + [vm] * len(thins),
        scratch_shapes=[
            pltpu.SMEM(seq_lens.shape, jnp.int32),
            area(1, rows, kind=jnp.int32),
            area(1, rows, kind=jnp.int32),
            area(rows, width),
            area(width, 5 * width),
            area(rows, width),
            area(width, rows),
            boxed,
            boxed,
            boxed,
            area(rows, rows),
            area(rows, rows),
            area(rows, width),
            area(width, rows),
            area(width, rows),
            area(4 * width, rows),
            area(width, rows),
            area(HEADS, head, rows),
            area(pairs, PAIR, rows),
            area(HEADS, head, rows),
            area(HEADS, rows, PAIR),
            area(HEADS, rows, PAIR),
            area(HEADS, ntile, QB, QB),
            area(HEADS, ntile, QB, QB),
            area(HEADS, head, rows, kind=F32),
            area(4 * width, rows),
            area(width, rows),
            area(pairs, PAIR, rows),
            area(PAIR // head, head, rows, kind=F32),
            area(max(1, blocks * (blocks - 1) // 2), PAIR, QB),
            dma((6,)),
            dma((n,)),
            dma((n,)),
            dma((n,)),
            dma((n,)),
            dma((len(thins) * bits,)),
            dma((len(thins) * bits,)),
        ]
        + bufs,
        compiler_params=pltpu.CompilerParams(
            collective_id=0, has_side_effects=True, vmem_limit_bytes=VMEM_LIMIT
        ),
        name="step",
    )(seq_lens, home, dest, events, weights, out_grad)
    if not direct:
        parts = [
            f.reshape(fold, per, f.shape[1]).transpose(1, 0, 2).reshape(per, fold * f.shape[1])
            for f in parts
        ]
    small = (*parts, momentum_in, momentum_out)
    return pl.pallas_call(
        functools.partial(finish_kernel, scale, columns, len(parts)),
        out_shape=[
            ev_shape,
            jax.ShapeDtypeStruct(momentum_in.shape, F32),
            jax.ShapeDtypeStruct(momentum_out.shape, F32),
        ],
        in_specs=[hbm] * (len(small) + 1),
        out_specs=[hbm] * 3,
        scratch_shapes=[
            area(rows, width),
            *(area(*x.shape, kind=F32) for x in small),
            area(*momentum_in.shape, kind=F32),
            area(*momentum_out.shape, kind=F32),
            dma((4,)),
            dma((6,)),
            dma((len(small),)),
        ],
        compiler_params=pltpu.CompilerParams(vmem_limit_bytes=VMEM_LIMIT),
        name="finish",
    )(ev, *small)


def solution(mesh):
    n = mesh.shape["dp"]
    row = P("dp", None)
    return jax.shard_map(
        functools.partial(shards, n),
        mesh=mesh,
        in_specs=(row, P("dp"), P("dp"), P("dp"), P(), row, row, row),
        out_specs=(row, row, row),
        check_vma=False,
    )
```

```python
import functools

import jax
import jax.numpy as jnp
from jax import lax
from jax.experimental import pallas as pl
from jax.experimental.pallas import tpu as pltpu
from jax.sharding import PartitionSpec as P

HEADS = 8
BLK = 512
QB = 256
PAIR = 128
NORM_EPS = 1e-05
DECAY = 0.9
MESH = pl.DeviceIdType.MESH
F32 = jnp.float32
BF16 = jnp.bfloat16
VMEM_LIMIT = 67 * 1000 * 1000
LAG = 4
BACK_LAG = 2
DEEP = 1
LATE = ((4, 0), (3, 1), (2, 2), (4, 1), (0, 4), (1, 4), (3, 2), (2, 3), (4, 2), (3, 3), (2, 4), (4, 3), (3, 4), (4, 4))
PLAN = (('fill', 3), ('fill', 1), ('msg', 3, 0), ('msg', 1, 0), ('msg', 3, 1), ('msg', 1, 1), ('msg', 3, 2), ('msg', 1, 2), ('msg', 3, 3), ('msg', 1, 3), ('fill', 0), ('fill', 2), ('own',), ('msg', 3, 4), ('msg', 1, 4), ('msg', 3, 5), ('msg', 1, 5), ('grad', 4), ('gone', 3, 0), ('gone', 1, 0), ('msg', 3, 6), ('msg', 1, 6), ('add', 2, 1), ('add', 3, 1), ('gone', 3, 1), ('gone', 1, 1), ('msg', 3, 7), ('msg', 1, 7), ('add', 4, 0), ('gone', 3, 2), ('gone', 1, 2), ('msg', 2, 0), ('msg', 0, 1), ('add', 0, 4), ('add', 1, 4), ('gone', 3, 3), ('gone', 1, 3), ('msg', 2, 1), ('msg', 0, 2), ('pick',), ('add', 2, 2), ('add', 4, 1), ('add', 3, 2), ('gone', 3, 4), ('gone', 1, 4), ('msg', 2, 2), ('msg', 0, 3), ('add', 2, 3), ('gone', 3, 5), ('gone', 1, 5), ('msg', 2, 3), ('msg', 0, 4), ('add', 4, 2), ('add', 3, 3), ('gone', 3, 6), ('gone', 1, 6), ('msg', 2, 4), ('msg', 0, 5), ('gone', 3, 7), ('gone', 1, 7), ('msg', 2, 5), ('msg', 0, 6), ('get', 1, True), ('add', 2, 4), ('add', 4, 3), ('add', 3, 4), ('gone', 2, 0), ('gone', 0, 1), ('msg', 2, 6), ('msg', 0, 7), ('gone', 2, 1), ('gone', 0, 2), ('msg', 2, 7), ('get', 0), ('get', 3), ('add', 4, 4), ('get', 2, False, True), ('gone', 2, 2), ('gone', 0, 3), ('gone', 2, 3), ('gone', 0, 4), ('gone', 2, 4), ('gone', 0, 5), ('gone', 2, 5), ('gone', 0, 6), ('gone', 2, 6), ('gone', 0, 7), ('gone', 2, 7))
WHOLE_PLAN = (
    *((what, k) for k in range(4) for what in ("fill", "start")),
    ("grad", 2),
    ("grad", 3),
    ("pick",),
    *(("add", chain, stage) for stage in (3, 4, 5, 6) for chain in (0, 1)),
    *(("add", chain, stage) for stage in range(7) for chain in (2, 3)),
    ("own",),
    ("get", 0, True),
    ("get", 1),
    ("get", 2),
    ("get", 3, False, True),
    *(("sent", k) for k in range(4)),
)


def dot_nn(a, b):
    return lax.dot_general(a, b, (((1,), (0,)), ((), ())), preferred_element_type=F32)


def dot_nt(a, b):
    return lax.dot_general(a, b, (((1,), (1,)), ((), ())), preferred_element_type=F32)


def chain_bits(bit_count, second):
    order = list(range(bit_count))
    if second and bit_count > 2:
        order[1], order[2] = order[2], order[1]
    return order


def slot_device(slot, n, bits):
    return sum(((slot // (n >> (rank + 1))) % 2) << bit for rank, bit in enumerate(bits))


def enter_all(n, me):
    barrier = pltpu.get_barrier_semaphore()

    def greet(i, carry):
        pl.semaphore_signal(barrier, inc=1, device_id=((me + i) % n,), device_id_type=MESH)
        return carry

    lax.fori_loop(1, n, greet, 0)
    return barrier


def flip(value, other, size):
    total = 0
    weight = 1
    while weight < size:
        total = total + (value // weight + other // weight) % 2 * weight
        weight *= 2
    return total


class Exchange:
    def __init__(self, n, me, group, src, dst, ssem, rsem):
        self.n, self.me, self.group = n, me, group
        self.src, self.dst, self.ssem, self.rsem = src, dst, ssem, rsem

    def chunk(self, k):
        return flip(self.me // self.group, k, self.n // self.group)

    def copy(self, k, j):
        peer = self.chunk(k) * self.group + flip(self.me % self.group, j, self.group)
        i = k * self.group + j
        return pltpu.make_async_remote_copy(
            src_ref=self.src.at[peer],
            dst_ref=self.dst.at[self.me],
            send_sem=self.ssem.at[i],
            recv_sem=self.rsem.at[i],
            device_id=(peer,),
            device_id_type=MESH,
        )

    def each(self, k, act):
        def go(j, carry):
            act(self.copy(k, j))
            return carry

        lax.fori_loop(1 if k == 0 else 0, self.group, go, 0)

    def start(self, k):
        self.each(k, lambda copy: copy.start())

    def sent(self, k):
        self.each(k, lambda copy: copy.wait_send())

    def arrived(self, k):
        self.each(k, lambda copy: copy.wait_recv())

    def finish(self, k):
        self.each(k, lambda copy: copy.wait())


def gather_matrix(slots_ref, out_ref):
    rows = out_ref.shape[0]
    wide = jnp.broadcast_to(slots_ref[...].astype(F32), (128, rows))
    column = jnp.transpose(wide)
    lane = lax.broadcasted_iota(jnp.int32, (rows, 128), 1).astype(F32)
    for j in range(rows // 128):
        out_ref[:, j * 128 : (j + 1) * 128] = jnp.where(
            column == lane + float(j * 128), 1.0, 0.0
        ).astype(BF16)


def scatter_chunk(slots_ref, start, size):
    rows = slots_ref.shape[1]
    place = lax.broadcasted_iota(jnp.int32, (size, rows), 0) + start
    return jnp.where(place == slots_ref[...], 1.0, 0.0).astype(BF16)


def same_owner(lens_ref, low, high):
    start = 0
    same = 0
    for j in range(lens_ref.shape[0]):
        blocks = (lens_ref[j] + BLK - 1) // BLK
        inside = jnp.where((start <= low) & (high < start + blocks), 1, 0)
        same = same + inside
        start = start + blocks
    return same


def order_block(height, base, width, n, per, bits, fold, turn):
    shape = (height, width)
    tall = per * fold
    place = lax.broadcasted_iota(jnp.int32, shape, 0) + base
    column = lax.broadcasted_iota(jnp.int32, shape, 1)
    slot = place // tall
    rest = place % tall
    device = jnp.zeros(shape, jnp.int32)
    for rank, bit in enumerate(bits):
        weight = n >> (rank + 1)
        device = device + ((slot // weight) % 2) * (1 << bit)
    hit = (column == device * per + rest % per) & (rest // per == turn)
    return jnp.where(hit, 1.0, 0.0).astype(BF16)


def step_kernel(n, direct, lens_hbm, home_hbm, dest_hbm, ev_hbm, w_hbm, og_hbm, *refs):
    chains = 5 if direct else 4
    out_ev, sums, refs = refs[0], refs[1 : 1 + chains], refs[1 + chains :]
    (
        lens_ref, home_ref, dest_ref, ev_ref,
        w_ref, og_ref, og_t, outbox, inbox, inbox2, pick, place, tok, tok_t, dmix_t,
        slope_t, gate_t, v_t, q_t, k_t, k_z, v_z, attn, slopes, att_t, hgrad_t, mixed_t,
        dout_t, acc, cross, lsem, ssem, rsem, ssem2, rsem2, hs, hr, *bufs,
    ) = refs
    me = lax.axis_index("dp")
    rows, width = ev_ref.shape
    cap = rows // n
    per = width // n
    fold = max(1, 16 // per)
    nq = rows // QB
    bits = n.bit_length() - 1
    group = QB // cap
    head = width // HEADS
    pairs = width // PAIR
    two = PAIR // head
    barrier = enter_all(n, me)
    loads = [
        pltpu.make_async_copy(src, dst, lsem.at[i])
        for i, (src, dst) in enumerate(
            (
                (home_hbm, home_ref),
                (ev_hbm, ev_ref),
                (dest_hbm, dest_ref),
                (og_hbm, og_ref),
                (w_hbm, w_ref),
                (lens_hbm, lens_ref),
            )
        )
    ]
    for load in loads:
        load.start()
    loads[0].wait()
    loads[1].wait()
    there = Exchange(n, me, group, outbox, inbox, ssem, rsem)
    back = Exchange(n, me, group, outbox, inbox2, ssem2, rsem2)

    for k in range(nq):
        at = there.chunk(k)
        part = dot_nn(scatter_chunk(home_ref, at * QB, QB), ev_ref[...]).astype(BF16)
        outbox[pl.ds(at * group, group)] = part.reshape(group, cap, width)
    pl.semaphore_wait(barrier, n - 1)
    for k in (*range(nq // 2, nq), *range(nq // 2 - 1, -1, -1)):
        there.start(k)
    inbox[me] = outbox[me]
    for load in loads[2:]:
        load.wait()
    gather_matrix(dest_ref, pick)

    def prepare(c, carry):
        r = pl.ds(pl.multiple_of(c * QB, QB), QB)
        place[r, :] = scatter_chunk(dest_ref, c * QB, QB)
        x = og_ref[r, :]
        og_t[:, r] = jnp.transpose(x)
        dmix_t[:, r] = (dot_nt(w_ref[:, 4 * width :], x) * 0.5).astype(BF16)
        return carry

    lax.fori_loop(0, nq, prepare, 0)

    def turn_w(c, carry):
        r = pl.ds(pl.multiple_of(c * QB, QB), QB)
        hgrad_t[r, :width] = jnp.transpose(w_ref[:, r]) * 0.5
        return carry

    lax.fori_loop(0, 4 * width // QB, turn_w, 0)

    blocks = rows // BLK
    links = [(i, j) for i in range(blocks) for j in range(i)]
    for x, (i, j) in enumerate(links):
        cross[x] = jnp.full((PAIR, QB), same_owner(lens_ref, j, i), jnp.int32).astype(F32).astype(BF16)

    def linked(value, qc, kc):
        i, j = qc * QB // BLK, kc * QB // BLK
        return value if i == j else value * cross[links.index((i, j))]

    arrivals = (*range(nq // 2 - 1, -1, -1), *range(nq // 2, nq))
    for k in arrivals:
        there.finish(k)
        at = there.chunk(k)
        box = inbox[pl.ds(at * group, group)].reshape(QB, width)
        part = dot_nn(pick[:, pl.ds(pl.multiple_of(at * QB, QB), QB)], box).astype(BF16)
        if k == arrivals[0]:
            tok[...] = part
        else:
            tok[...] += part

    lane = lax.broadcasted_iota(jnp.int32, (1, PAIR), 1) // head
    picks = [jnp.where(lane == h, 1.0, 0.0).astype(BF16) for h in range(two)]

    def project(c, carry):
        r = pl.ds(pl.multiple_of(c * QB, QB), QB)
        x = tok[r, :]
        for g in range(4):
            rs = slice(g * width, (g + 1) * width)
            u = dot_nt(hgrad_t[rs, :width], x)
            w = jnp.tanh(u) + 1.0
            a = u * w
            low = a.astype(BF16)
            wb = w.astype(BF16)
            slope_t[rs, r] = wb + low * (2.0 - wb)
            if g == 0:
                gate_t[:, r] = low
            elif g == 2:
                q_t[:, :, r] = (low * (0.5 * head**-0.5)).reshape(pairs, PAIR, QB)
            else:
                here, flat = (v_t, v_z) if g == 1 else (k_t, k_z)
                here[:, :, r] = low.reshape(HEADS, head, QB)
                for p in range(pairs):
                    tall = jnp.transpose(low[p * PAIR : (p + 1) * PAIR])
                    for h in range(two):
                        flat[p * two + h, r, :] = tall * picks[h]
        return carry

    lax.fori_loop(0, nq, project, 0)

    tiles = [(qc, kc) for qc in range(nq) for kc in range(qc + 1)]
    low_i = lax.broadcasted_iota(jnp.int32, (QB, QB), 0)
    high_i = lax.broadcasted_iota(jnp.int32, (QB, QB), 1)

    def span(c):
        return slice(c * QB, (c + 1) * QB)

    def forward(p, carry):
        tri = jnp.where(low_i <= high_i, 1.0, 0.0).astype(BF16)
        work = [(h, qc, kc) for h in range(two) for qc, kc in tiles]
        held = {}
        out = None
        for i in range(len(work) + LAG):
            if i < len(work):
                h, qc, kc = work[i]
                q = linked(q_t[p, :, span(qc)], qc, kc)
                held[i] = dot_nn(k_z[p * two + h, span(kc), :], q)
            if i < LAG:
                continue
            h, qc, kc = work[i - LAG]
            u = held.pop(i - LAG)
            g = p * two + h
            w = jnp.tanh(u) + 1.0
            a = (u * w).astype(BF16)
            wb = w.astype(BF16)
            if qc == kc:
                a = a * tri
                wb = wb * tri
            attn[g, tiles.index((qc, kc))] = a
            slopes[g, tiles.index((qc, kc))] = wb
            o = dot_nn(v_t[g, :, span(kc)], a)
            out = o if kc == 0 else out + o
            if qc == kc:
                att_t[g, :, span(qc)] = out
        return carry

    lax.fori_loop(0, pairs, forward, 0)

    def norm(c, carry):
        r = pl.ds(pl.multiple_of(c * 128, 128), 128)
        x = att_t[:, :, r].reshape(width, 128)
        centred = x - jnp.mean(x, axis=0, keepdims=True)
        spread = jnp.mean(centred * centred, axis=0, keepdims=True)
        inv = lax.rsqrt(spread + NORM_EPS)
        unit = centred * inv
        g = gate_t[:, r].astype(F32)
        mixed_t[:, r] = (unit * g).astype(BF16)
        dm = dmix_t[:, r].astype(F32)
        hgrad_t[:width, r] = (dm * unit * slope_t[:width, r].astype(F32)).astype(BF16)
        dn = dm * g
        mean_a = jnp.mean(dn, axis=0, keepdims=True)
        mean_b = jnp.mean(dn * unit, axis=0, keepdims=True)
        dout_t[:, :, r] = (
            (inv * (dn - mean_a - unit * mean_b)).astype(BF16).reshape(pairs, PAIR, 128)
        )
        return carry

    lax.fori_loop(0, rows // 128, norm, 0)

    sources = bufs[:chains]
    hops = bufs[chains:]
    orders = [chain_bits(bits, chain in (1, 2)) for chain in range(chains)]

    def hop(chain, stage):
        bit = orders[chain][stage]
        mine = (me // (1 << bit)) % 2
        peer = me + (1 - 2 * mine) * (1 << bit)
        cur = sources[chain] if stage == 0 else hops[chain * bits + stage - 1]
        got = hops[chain * bits + stage]
        half = cur.shape[0] // 2
        copy = pltpu.make_async_remote_copy(
            src_ref=cur.at[pl.ds((1 - mine) * half, half)],
            dst_ref=got,
            send_sem=hs.at[chain * bits + stage],
            recv_sem=hr.at[chain * bits + stage],
            device_id=(peer,),
            device_id_type=MESH,
        )
        return copy, cur.at[pl.ds(mine * half, half)], got

    columns = chain_columns(width, direct)

    def advance(chain, stage):
        copy, kept, got = hop(chain, stage)
        copy.wait()
        total = kept[...].astype(F32) + got[...].astype(F32)
        if stage == bits - 1:
            sums[chain][...] = total
        else:
            got[...] = total.astype(BF16)
            hop(chain, stage + 1)[0].start()

    def weight_grad(chain):
        order = orders[chain]
        if direct:
            pieces = [
                (start + j, PAIR) for start, size in columns[chain] for j in range(0, size, PAIR)
            ]
            for x in range(0, len(pieces), 2):
                some = pieces[x : x + 2]
                if chain == 1:
                    right = [og_ref[:, lo : lo + size] for lo, size in some]
                    part = dot_nn(mixed_t[...], jnp.concatenate(right, axis=1))
                else:
                    right = [hgrad_t[lo : lo + size, :] for lo, size in some]
                    part = dot_nt(tok_t[...], jnp.concatenate(right, axis=0))
                part = part.astype(BF16)
                cols = slice(x * PAIR, x * PAIR + part.shape[1])
                for slot in range(n):
                    d = slot_device(slot, n, order)
                    sources[chain][slot * per : (slot + 1) * per, cols] = part[d * per : (d + 1) * per]
        else:
            base, size = columns[chain][0]
            thin = size // fold
            step = QB if thin % QB == 0 else thin
            strip = 128

            def fold_rows(x, carry):
                lo = pl.multiple_of(x * strip, strip)
                spot = pl.ds(lo, strip)
                for turn in range(fold):
                    mat = order_block(strip, lo, width, n, per, order, fold, turn)
                    if chain == 1:
                        left = dot_nn(mat, mixed_t[...]).astype(BF16)
                    else:
                        left = dot_nt(mat, tok[...]).astype(BF16)
                    for j in range(thin // step):
                        start = base + turn * thin + j * step
                        if chain == 1:
                            part = dot_nn(left, og_ref[:, start : start + step])
                        else:
                            part = dot_nt(left, hgrad_t[start : start + step, :])
                        cols = slice(j * step, (j + 1) * step)
                        if turn == 0:
                            sources[chain][spot, cols] = part.astype(BF16)
                        else:
                            sources[chain][spot, cols] += part.astype(BF16)
                return carry

            lax.fori_loop(0, n * per * fold // strip, fold_rows, 0)
        hop(chain, 0)[0].start()

    if direct:
        for c in range(nq):
            tok_t[:, span(c)] = jnp.transpose(tok[span(c), :])
    weight_grad(0)
    weight_grad(1)

    def backward(p, carry):
        work = [(h, qc, kc) for h in range(two) for kc in range(nq) for qc in range(kc, nq)]
        held = {}
        ready = {}
        dk = dv = None
        for i in range(len(work) + BACK_LAG + DEEP):
            if i < len(work):
                h, qc, kc = work[i]
                d = linked(dout_t[p, :, span(qc)], qc, kc)
                held[i] = dot_nn(v_z[p * two + h, span(kc), :], d)
            j = i - BACK_LAG
            if 0 <= j < len(work):
                h, qc, kc = work[j]
                a = attn[p * two + h, tiles.index((qc, kc))]
                wb = slopes[p * two + h, tiles.index((qc, kc))]
                ready[j] = held.pop(j).astype(BF16) * (wb + a * (2.0 - wb))
            j = i - BACK_LAG - DEEP
            if j < 0:
                continue
            h, qc, kc = work[j]
            ds = ready.pop(j)
            g = p * two + h
            mine = slice(h * head, (h + 1) * head)
            dq = dot_nn(k_t[g, :, span(kc)], ds)
            if kc == 0:
                acc[h, :, span(qc)] = dq
            else:
                acc[h, :, span(qc)] += dq
            more_k = dot_nt(q_t[p, mine, span(qc)], ds)
            more_v = dot_nt(dout_t[p, mine, span(qc)], attn[g, tiles.index((qc, kc))])
            dk = more_k if qc == kc else dk + more_k
            dv = more_v if qc == kc else dv + more_v
            if qc == nq - 1:
                for grp, val in ((1, dv), (3, dk)):
                    rs = pl.ds(pl.multiple_of(grp * width + p * PAIR + h * head, head), head)
                    hgrad_t[rs, span(kc)] = (
                        val.astype(BF16).astype(F32) * slope_t[rs, span(kc)].astype(F32)
                    ).astype(BF16)
            if kc == qc:
                rs = pl.ds(pl.multiple_of(2 * width + p * PAIR + h * head, head), head)
                full = (acc[h, :, span(qc)] * (0.5 * head**-0.5)).astype(BF16).astype(F32)
                hgrad_t[rs, span(qc)] = (full * slope_t[rs, span(qc)].astype(F32)).astype(BF16)

        @pl.when(p == 0)
        def _():
            advance(0, 0)
            advance(1, 0)

        if direct:

            @pl.when(p == pairs - 3)
            def _():
                weight_grad(2)
                advance(0, 1)
                advance(1, 1)

        @pl.when(p == pairs - 2)
        def _():
            if direct:
                advance(2, 0)
                weight_grad(3)
                advance(0, 2)
                advance(1, 2)

        @pl.when(p == pairs - 1)
        def _():
            if direct:
                advance(3, 0)
                advance(0, 3)
                advance(1, 3)
            else:
                for stage in (1, 2):
                    advance(0, stage)
                    advance(1, stage)

        return carry

    lax.fori_loop(0, pairs, backward, 0)

    def tokens_back(c, carry):
        r = pl.ds(pl.multiple_of(c * QB, QB), QB)
        dmix_t[:, r] = (
            og_t[:, r].astype(F32) + dot_nn(w_ref[:, : 4 * width], hgrad_t[:, r])
        ).astype(BF16)
        return carry

    lax.fori_loop(0, nq, tokens_back, 0)

    if direct:
        pass
    def fill_back(k):
        at = back.chunk(k)
        r = pl.ds(pl.multiple_of(at * QB, QB), QB)
        part = dot_nt(place[r, :], dmix_t[...]).astype(BF16)
        outbox[pl.ds(at * group, group)] = part.reshape(group, cap, width)

    stores = []

    def collect(k, first=False, last=False):
        back.arrived(k)
        at = back.chunk(k)
        box = inbox2[pl.ds(at * group, group)].reshape(QB, width)
        cols = pl.ds(pl.multiple_of(at * QB, QB), QB)
        if not last:
            part = dot_nn(pick[:, cols], box).astype(BF16)
            tok[...] = part if first else tok[...] + part
            return
        for c in range(nq):
            tok[span(c), :] += dot_nn(pick[span(c), cols], box).astype(BF16)
            stores.append(
                pltpu.make_async_copy(tok.at[span(c)], out_ev.at[span(c)], lsem.at[c])
            )
            stores[-1].start()

    plan = PLAN if direct else WHOLE_PLAN
    for what, *args in plan:
        if what == "fill":
            fill_back(*args)
        elif what == "start":
            back.start(*args)
        elif what == "sent":
            back.sent(*args)
        elif what == "msg":
            back.copy(*args).start()
        elif what == "gone":
            back.copy(*args).wait_send()
        elif what == "get":
            collect(*args)
        elif what == "own":
            inbox2[me] = outbox[me]
        elif what == "grad":
            weight_grad(*args)
        elif what == "pick":
            gather_matrix(home_ref, pick)
        else:
            advance(*args)
    inbox2[me] = outbox[me]
    for store in stores:
        store.wait()


def chain_columns(width, direct):
    half = width // 2
    if not direct:
        return [[(0, width)], [(0, width)], [(width, 3 * half)], [(width + 3 * half, 3 * half)]]
    parts = ((0, half), (half, PAIR), (half + PAIR, PAIR))
    late = [[(width * g + at, size) for g in (1, 2, 3)] for at, size in parts]
    return [[(0, width)], [(0, width)], *late]


def finish_kernel(scale, columns, count, *refs):
    wide, spots, scratch = refs[: count + 3], refs[count + 3 : count + 6], refs[count + 6 :]
    ev_hbm, *small = wide
    held, *near, ni_ref, no_ref, isem, osem, psem = scratch
    loads, stores = [], []
    parts = osem.shape[0] - 2
    size = held.shape[0] // parts
    for i in range(parts):
        r = pl.ds(i * size, size)
        loads.append(pltpu.make_async_copy(ev_hbm.at[r], held.at[r], isem.at[i]))
        stores.append(pltpu.make_async_copy(held.at[r], spots[0].at[r], osem.at[i]))
    other = [
        pltpu.make_async_copy(src, dst, psem.at[i]) for i, (src, dst) in enumerate(zip(small, near))
    ]
    for load in [*other, *loads]:
        load.start()
    for load in other:
        load.wait()
    *sums, mi_ref, mo_ref = near
    no_ref[...] = DECAY * mo_ref[...] + scale * sums[1][...]
    for chain in range(count):
        if chain == 1:
            continue
        at = 0
        for start, span in columns[chain]:
            cols = slice(start, start + span)
            ni_ref[:, cols] = DECAY * mi_ref[:, cols] + scale * sums[chain][:, at : at + span]
            at += span
    stores.append(pltpu.make_async_copy(ni_ref, spots[1], osem.at[parts]))
    stores.append(pltpu.make_async_copy(no_ref, spots[2], osem.at[parts + 1]))
    stores[-1].start()
    stores[-2].start()
    for load, store in zip(loads, stores):
        load.wait()
        store.start()
    for store in stores:
        store.wait()


def shards(n, events, home_slot, dest_slot, seq_lens, weights, out_grad, momentum_in, momentum_out):
    rows, width = events.shape
    cap = rows // n
    bits = n.bit_length() - 1
    per = width // n
    fold = max(1, 16 // per)
    tall = per * fold
    direct = fold == 1
    nq = rows // QB
    pairs = width // PAIR
    head = width // HEADS
    scale = (n * rows) ** (-0.5)
    home = home_slot.reshape(1, rows)
    dest = dest_slot.reshape(1, rows)
    vm = pl.BlockSpec(memory_space=pltpu.VMEM)
    sm = pl.BlockSpec(memory_space=pltpu.SMEM)
    hbm = pl.BlockSpec(memory_space=pl.ANY)
    dma = pltpu.SemaphoreType.DMA
    columns = chain_columns(width, direct)
    wides = [sum(size for _, size in cols) for cols in columns]
    thins = [w // fold for w in wides]
    bufs = [pltpu.VMEM((n * tall, t), BF16) for t in thins]
    for t in thins:
        for stage in range(bits):
            bufs.append(pltpu.VMEM((n * tall >> (stage + 1), t), BF16))

    def area(*shape, kind=BF16):
        return pltpu.VMEM(shape, kind)

    boxed = area(n, cap, width)
    ntile = nq * (nq + 1) // 2
    blocks = rows // BLK
    ev_shape = jax.ShapeDtypeStruct(events.shape, BF16)
    ev, *parts = pl.pallas_call(
        functools.partial(step_kernel, n, direct),
        out_shape=[ev_shape] + [jax.ShapeDtypeStruct((tall, t), F32) for t in thins],
        in_specs=[hbm] * 6,
        out_specs=[hbm] + [vm] * len(thins),
        scratch_shapes=[
            pltpu.SMEM(seq_lens.shape, jnp.int32),
            area(1, rows, kind=jnp.int32),
            area(1, rows, kind=jnp.int32),
            area(rows, width),
            area(width, 5 * width),
            area(rows, width),
            area(width, rows),
            boxed,
            boxed,
            boxed,
            area(rows, rows),
            area(rows, rows),
            area(rows, width),
            area(width, rows),
            area(width, rows),
            area(4 * width, rows),
            area(width, rows),
            area(HEADS, head, rows),
            area(pairs, PAIR, rows),
            area(HEADS, head, rows),
            area(HEADS, rows, PAIR),
            area(HEADS, rows, PAIR),
            area(HEADS, ntile, QB, QB),
            area(HEADS, ntile, QB, QB),
            area(HEADS, head, rows, kind=F32),
            area(4 * width, rows),
            area(width, rows),
            area(pairs, PAIR, rows),
            area(PAIR // head, head, rows, kind=F32),
            area(max(1, blocks * (blocks - 1) // 2), PAIR, QB),
            dma((6,)),
            dma((n,)),
            dma((n,)),
            dma((n,)),
            dma((n,)),
            dma((len(thins) * bits,)),
            dma((len(thins) * bits,)),
        ]
        + bufs,
        compiler_params=pltpu.CompilerParams(
            collective_id=0, has_side_effects=True, vmem_limit_bytes=VMEM_LIMIT
        ),
        name="step",
    )(seq_lens, home, dest, events, weights, out_grad)
    if not direct:
        parts = [
            f.reshape(fold, per, f.shape[1]).transpose(1, 0, 2).reshape(per, fold * f.shape[1])
            for f in parts
        ]
    small = (*parts, momentum_in, momentum_out)
    return pl.pallas_call(
        functools.partial(finish_kernel, scale, columns, len(parts)),
        out_shape=[
            ev_shape,
            jax.ShapeDtypeStruct(momentum_in.shape, F32),
            jax.ShapeDtypeStruct(momentum_out.shape, F32),
        ],
        in_specs=[hbm] * (len(small) + 1),
        out_specs=[hbm] * 3,
        scratch_shapes=[
            area(rows, width),
            *(area(*x.shape, kind=F32) for x in small),
            area(*momentum_in.shape, kind=F32),
            area(*momentum_out.shape, kind=F32),
            dma((4,)),
            dma((6,)),
            dma((len(small),)),
        ],
        compiler_params=pltpu.CompilerParams(vmem_limit_bytes=VMEM_LIMIT),
        name="finish",
    )(ev, *small)


def solution(mesh):
    n = mesh.shape["dp"]
    row = P("dp", None)
    return jax.shard_map(
        functools.partial(shards, n),
        mesh=mesh,
        in_specs=(row, P("dp"), P("dp"), P("dp"), P(), row, row, row),
        out_specs=(row, row, row),
        check_vma=False,
    )
```
